256 devices in a mesh: dp: 8 (over x, core), shard: 32 (over z, y).
Axes of the slice: x: 4, y: 4, z: 8, core: 2. Of those that a mesh axis runs over, the one named last changes fastest.
Arguments:
- table: float32 [65536, 128], P('shard'), may hold values from -6 to 6
- cross_weight: bfloat16 [1024, 1024], replicated, may hold values from -0.1875 to 0.1875
- cross_bias: float32 [1024], replicated, may hold values from -3 to 3
- top_weight: bfloat16 [1024, 512], replicated, may hold values from -0.1875 to 0.1875
- top_bias: float32 [512], replicated, may hold values from -3 to 3
- out_weight: float32 [512], replicated, may hold values from -0.25 to 0.25
- wanted: int32 [256, 32, 128], P(('dp', 'shard')), may hold values from 0 to 2047, as said below
- slots: int32 [131072, 8, 4], P(('dp', 'shard')), may hold values from 0 to 4095
- lengths: int32 [131072, 8], P(('dp', 'shard')), may hold values from 1 to 4
- logit_grad: float32 [131072], P(('dp', 'shard')), may hold values from -6 to 6
Outputs:
- logits: float32 [131072], P(('dp', 'shard'))
- grad_cross: float32 [1024, 1024], replicated
- grad_top: float32 [1024, 512], replicated
- grad_cross_bias: float32 [1024], replicated
- grad_top_bias: float32 [512], replicated
- grad_out: float32 [512], replicated
- table_grad: float32 [65536, 128], P('shard')
The draws below stay inside these ranges and needn't reach their ends.
Inputs may be any that keep to these rules, and one draw needn't show every extreme that they name: `wanted`: the 128 rows that one device fetches from one owner are distinct.
All inputs are finite; a program needn't handle non-finite values.
Results may differ from the reference program's by a relative error of at most 0.0084.
Values sent between devices are 32-bit elements; how exact they have to be, the bound alone decides.
A program may use at most 128 MiB of HBM per device.

```python
import jax
import jax.numpy as jnp
from jax import lax

D_EMB = 128
FEATS = 8
TOP = 512
BAG = 4
ROWS_DEV = 2048
CAP = 128
SAMPLES_DEV = 512
WIDTH = 1024
TABLE_ROWS = 65536
SAMPLES = 131072
N_SHARD = 32
DEVICES = 256


def draw_wanted(key, part):
    order_keys = jax.random.split(jax.random.fold_in(key, 11), N_SHARD)
    ranking = jax.vmap(lambda one: jax.random.permutation(one, ROWS_DEV))(order_keys).astype(jnp.int32)
    divisor = ranking // 8 + 1
    raw_scores = jax.random.randint(jax.random.fold_in(key, 12), (DEVICES, N_SHARD, ROWS_DEV), 0, 65536, dtype=jnp.int32)
    scores = raw_scores // divisor[None] * ROWS_DEV + jnp.arange(ROWS_DEV, dtype=jnp.int32)[None, None, :]
    unused, picked = lax.top_k(scores, CAP)
    return picked.astype(jnp.int32)


def place_ends(result, stream_key, smallest, largest):
    index_at = [jax.random.randint(jax.random.fold_in(stream_key, axis), (), 0, length) for axis, length in enumerate(result.shape)]
    widest = result.shape.index(max(result.shape))
    neighbour = index_at[:widest] + [(index_at[widest] + 1) % result.shape[widest]] + index_at[widest + 1:]
    return result.at[tuple(index_at)].set(smallest).at[tuple(neighbour)].set(largest)


def block_scale(stream_key, extent, cuts, low, largest):
    level = 1.0
    for dim, shards_of in cuts:
        draws = jax.random.uniform(jax.random.fold_in(jax.random.fold_in(stream_key, 6), dim), (shards_of,), jnp.float32, low / len(cuts), largest / len(cuts))
        level = level * jnp.repeat(jnp.exp(draws), extent[dim] // shards_of).reshape((-1,) + (1,) * (len(extent) - 1 - dim))
    return level


def bell_draw(own_key, extent, deviation, reach, cuts=(), held_as=jnp.bfloat16):
    loudness = block_scale(own_key, extent, cuts, -0.22, 0.18) if cuts else 1.0
    drawn = jax.random.normal(own_key, extent, jnp.float32) * deviation * loudness
    return jnp.minimum(jnp.maximum(drawn, -reach), reach).astype(held_as)


def setup_inputs(seed: int = 0) -> dict:
    streams_of = jax.random.split(jax.random.key(seed), 11)
    return {
        "table": bell_draw(streams_of[0], (TABLE_ROWS, D_EMB), 1.0, 6.0, ((0, 32),), jnp.float32),
        "cross_weight": bell_draw(streams_of[1], (WIDTH, WIDTH), WIDTH ** -0.5, 0.1875),
        "cross_bias": bell_draw(streams_of[2], (WIDTH,), 0.5, 3.0, (), jnp.float32),
        "top_weight": bell_draw(streams_of[3], (WIDTH, TOP), WIDTH ** -0.5, 0.1875),
        "top_bias": bell_draw(streams_of[4], (TOP,), 0.5, 3.0, (), jnp.float32),
        "out_weight": bell_draw(streams_of[5], (TOP,), TOP ** -0.5, 0.25, (), jnp.float32),
        "wanted": draw_wanted(jax.random.fold_in(streams_of[10], 71), 0),
        "slots": place_ends(jax.random.randint(streams_of[7], (SAMPLES, FEATS, BAG), 0, N_SHARD * CAP), jax.random.fold_in(streams_of[7], 1), 0, (N_SHARD * CAP) - 1).astype(jnp.int32),
        "lengths": place_ends(jax.random.randint(streams_of[8], (SAMPLES, FEATS), 1, BAG + 1), jax.random.fold_in(streams_of[8], 1), 1, BAG).astype(jnp.int32),
        "logit_grad": bell_draw(streams_of[9], (SAMPLES,), 1.0, 6.0, ((0, 256),), jnp.float32),
    }


def reference(table, cross_weight, cross_bias, top_weight, top_bias, out_weight, wanted, slots, lengths, logit_grad):
    owners = (jnp.arange(N_SHARD, dtype=jnp.int32) * ROWS_DEV)[:, None]
    devices = wanted.shape[0]
    slot_dev = slots.reshape(devices, SAMPLES_DEV, FEATS, BAG)
    len_dev = lengths.reshape(devices, SAMPLES_DEV, FEATS)
    grad_dev = logit_grad.reshape(devices, SAMPLES_DEV)

    def device_step(carry, inputs):
        g_cross, g_top, g_cbias, g_tbias, g_out, t_grad = carry
        want_here, slot_here, len_here, cot = inputs
        rowmap = (owners + want_here).reshape(-1).astype(jnp.int32)
        row_ids = rowmap[slot_here]
        live = (jnp.arange(BAG, dtype=jnp.int32)[None, None, :] < len_here[:, :, None]).astype(jnp.float32)
        gathered = table[row_ids]
        pooled = jnp.sum(gathered * live[..., None], axis=2)
        x0 = pooled.reshape(SAMPLES_DEV, FEATS * D_EMB).astype(jnp.bfloat16)
        xfull = x0.astype(jnp.float32)
        yval = jnp.dot(x0, cross_weight, preferred_element_type=jnp.float32) + cross_bias
        hidden = (xfull * yval + xfull).astype(jnp.bfloat16)
        zval = jnp.dot(hidden, top_weight, preferred_element_type=jnp.float32) + top_bias
        sig = jax.nn.sigmoid(zval)
        uval = zval * sig
        logit = jnp.dot(uval, out_weight, precision=lax.Precision.HIGHEST)
        g_out = g_out + jnp.dot(cot, uval, precision=lax.Precision.HIGHEST)
        dz = cot[:, None] * out_weight[None, :] * (sig * (1.0 + zval * (1.0 - sig)))
        dzb = dz.astype(jnp.bfloat16)
        g_top = g_top + jnp.dot(hidden.T, dzb, preferred_element_type=jnp.float32)
        g_tbias = g_tbias + jnp.sum(dz, axis=0)
        dh = jnp.dot(dzb, top_weight.T, preferred_element_type=jnp.float32)
        dy = dh * xfull
        dyb = dy.astype(jnp.bfloat16)
        g_cross = g_cross + jnp.dot(x0.T, dyb, preferred_element_type=jnp.float32)
        g_cbias = g_cbias + jnp.sum(dy, axis=0)
        dx = dh * (yval + 1.0) + jnp.dot(dyb, cross_weight.T, preferred_element_type=jnp.float32)
        contrib = dx.reshape(SAMPLES_DEV, FEATS, 1, D_EMB) * live[..., None]
        t_grad = t_grad.at[row_ids.reshape(-1)].add(contrib.reshape(-1, D_EMB))
        return (g_cross, g_top, g_cbias, g_tbias, g_out, t_grad), logit

    width = FEATS * D_EMB
    init = (jnp.zeros((width, width), jnp.float32), jnp.zeros((width, TOP), jnp.float32),
            jnp.zeros((width,), jnp.float32), jnp.zeros((TOP,), jnp.float32),
            jnp.zeros((TOP,), jnp.float32), jnp.zeros(table.shape, jnp.float32))
    final, logit_all = lax.scan(device_step, init, (wanted, slot_dev, len_dev, grad_dev))
    g_cross, g_top, g_cbias, g_tbias, g_out, t_grad = final
    return (logit_all.reshape(-1), g_cross, g_top, g_cbias, g_tbias, g_out, t_grad)
```

```python
import functools
import jax
import jax.numpy as jnp
from jax import lax
from jax.experimental import pallas as pl
from jax.experimental.pallas import tpu as pltpu
from jax.sharding import PartitionSpec as P

VMEM_BIG = 60 * 1024 * 1024


def peer_of(k, me, ny, nz):
    j = k // ny
    dz = nz // 2 + (j // 2 + j % 2) * (1 - 2 * (j % 2))
    dy = (k + 1) % ny
    z = (me // ny + dz + nz) % nz
    y = (me % ny + dy) % ny
    return z * ny + y


def fetch_kernel(n, ny, wanted, table, cache, ids_in, ids_sm, sendbuf,
                 id_send, id_recv, row_send, row_recv, sm_sem):
    nz = n // ny
    cap = wanted.shape[2]
    me = lax.axis_index("shard")
    barrier = pltpu.get_barrier_semaphore()

    @pl.loop(0, n - 1)
    def _(k):
        pl.semaphore_signal(barrier, inc=1, device_id={"shard": peer_of(k, me, ny, nz)})

    pl.semaphore_wait(barrier, n - 1)

    def id_copy(p):
        return pltpu.make_async_remote_copy(
            src_ref=wanted.at[p], dst_ref=ids_in.at[me], send_sem=id_send.at[p],
            recv_sem=id_recv.at[me], device_id={"shard": p})

    def id_arrival(p):
        return pltpu.make_async_remote_copy(
            src_ref=wanted.at[p], dst_ref=ids_in.at[p], send_sem=id_send.at[p],
            recv_sem=id_recv.at[p], device_id={"shard": p})

    def row_copy(p):
        return pltpu.make_async_remote_copy(
            src_ref=sendbuf.at[p], dst_ref=cache.at[me], send_sem=row_send.at[p],
            recv_sem=row_recv.at[me], device_id={"shard": p})

    def row_arrival(p):
        return pltpu.make_async_remote_copy(
            src_ref=sendbuf.at[p], dst_ref=cache.at[p], send_sem=row_send.at[p],
            recv_sem=row_recv.at[p], device_id={"shard": p})

    @pl.loop(0, n - 1)
    def _(k):
        id_copy(peer_of(k, me, ny, nz)).start()

    ids_in[me] = wanted[me]

    @pl.loop(0, n - 1)
    def _(k):
        id_arrival(peer_of(k, me, ny, nz)).wait_recv()

    to_smem = pltpu.make_async_copy(ids_in, ids_sm, sm_sem)
    to_smem.start()
    to_smem.wait()

    def serve(p, out):
        @pl.loop(0, cap // 16)
        def _(t):
            for i in range(16):
                row = t * 16 + i
                out[p, pl.ds(row, 1), :] = table[pl.ds(ids_sm[p, 0, row], 1), :]

    @pl.loop(0, n - 1)
    def _(k):
        p = peer_of(k, me, ny, nz)
        serve(p, sendbuf)
        row_copy(p).start()

    serve(me, cache)

    @pl.loop(0, n - 1)
    def _(k):
        p = peer_of(k, me, ny, nz)
        row_arrival(p).wait_recv()

    @pl.loop(0, n - 1)
    def _(k):
        p = peer_of(k, me, ny, nz)
        id_copy(p).wait_send()
        row_copy(p).wait_send()


def fetch(wanted, table, ny):
    n, cap = wanted.shape
    emb = table.shape[1]
    vm = pl.BlockSpec(memory_space=pltpu.VMEM)
    cache, served = pl.pallas_call(
        functools.partial(fetch_kernel, n, ny),
        out_shape=[
            jax.ShapeDtypeStruct((n, cap, emb), jnp.float32),
            jax.ShapeDtypeStruct((n, 1, cap), jnp.int32),
        ],
        in_specs=[vm, vm],
        out_specs=[vm, vm],
        scratch_shapes=[
            pltpu.SMEM((n, 1, cap), jnp.int32),
            pltpu.VMEM((n, cap, emb), jnp.float32),
            pltpu.SemaphoreType.DMA((n,)),
            pltpu.SemaphoreType.DMA((n,)),
            pltpu.SemaphoreType.DMA((n,)),
            pltpu.SemaphoreType.DMA((n,)),
            pltpu.SemaphoreType.DMA,
        ],
        compiler_params=pltpu.CompilerParams(
            collective_id=0, has_side_effects=True, vmem_limit_bytes=VMEM_BIG),
        name="fetch_rows",
    )(wanted.reshape(n, 1, cap), table)
    return cache, served

F32, BF16, I32 = jnp.float32, jnp.bfloat16, jnp.int32


def dot(a, b, dims):
    return lax.dot_general(a, b, (dims, ((), ())), preferred_element_type=F32)


NN = ((1,), (0,))
NT = ((1,), (1,))
TN = ((0,), (0,))


def split(x):
    hi = x.astype(BF16)
    lo = (x - hi.astype(F32)).astype(BF16)
    return jnp.concatenate([hi, lo], axis=1)


def nibble_scale(o):
    k = o % 8
    s = jnp.where((k & 1) == 1, F32(2.0**-4), F32(1.0))
    s = s * jnp.where((k & 2) == 2, F32(2.0**-8), F32(1.0))
    return s * jnp.where((k & 4) == 4, F32(2.0**-16), F32(1.0))


def key_codes(slots, lengths, b):
    slot = slots[:, b, :]
    owner = slot >> 7
    code = jnp.where(lengths[...] > b, (slot & 127) + ((owner >> 3) << 7), -1)
    return code, jnp.left_shift(jnp.ones_like(owner), (owner & 7) << 2)


def local_kernel(cache, slots, lengths, cot, cw, cb, tw, tb, ow,
                 logits, g_cross, g_top, g_cb, g_tb, g_ow, slot_grads,
                 words, wordst, colcode, colbit, rowcode, rowbit, acc, chl, x0, y, h, z, dzb, dyb, dh, dxhl):
    feats, bag, samples = slots.shape
    owners, cap, emb = cache.shape
    width, top = tw.shape
    groups = words.shape[0]

    for b in range(bag):
        code, bit = key_codes(slots, lengths, b)
        rowcode[pl.ds(b * feats, feats), :] = code
        rowbit[pl.ds(b * feats, feats), :] = bit
    colcode[...] = rowcode[...].T
    colbit[...] = rowbit[...].T

    lane = lax.broadcasted_iota(I32, (samples, cap), 1)
    for f in range(feats):
        sums = [jnp.zeros((samples, cap), I32)] * groups
        for b in range(bag):
            col = b * feats + f
            code = jnp.broadcast_to(colcode[:, col:col + 1], (samples, cap)) - lane
            bit = jnp.broadcast_to(colbit[:, col:col + 1], (samples, cap))
            for w in range(groups):
                sums[w] = sums[w] + jnp.where(code == w * cap, bit, 0)
        for w in range(groups):
            words[w, f] = sums[w]

    for o in range(owners):
        scale = 2.0 ** -(4 * (o % 8))
        chl[pl.ds(o * cap, cap), :] = split(cache[o] * scale)

    per = 4

    @pl.loop(0, owners // per)
    def _(g):
        w = g // 2
        rhs = chl[pl.ds(g * per * cap, per * cap), :]

        @pl.loop(0, feats)
        def _(f):
            word = words[w, f]
            tiles = []
            for i in range(per):
                mask = jnp.left_shift(jnp.int32(15), ((g % 2) * per + i) * 4)
                tiles.append((word & mask).astype(F32).astype(BF16))
            part = dot(jnp.concatenate(tiles, axis=1), rhs, NN)

            @pl.when(g == 0)
            def _():
                acc[f] = part

            @pl.when(g > 0)
            def _():
                acc[f] += part

    for f in range(feats):
        x0[:, f * emb:(f + 1) * emb] = (acc[f, :, :emb] + acc[f, :, emb:]).astype(BF16)

    step = 256

    @pl.loop(0, width // step)
    def _(j):
        c = pl.ds(pl.multiple_of(j * step, step), step)
        yv = dot(x0[...], cw[:, c], NN) + cb[:, c]
        y[:, c] = yv
        xf = x0[:, c].astype(F32)
        h[:, c] = (xf * yv + xf).astype(BF16)

    cotb = jnp.broadcast_to(cot[...], (128, samples)).T
    lsum = jnp.zeros((samples, 128), F32)
    for j in range(top // step):
        c = pl.ds(j * step, step)
        zv = dot(h[...], tw[:, c], NN) + tb[:, c]
        sig = jax.nn.sigmoid(zv)
        u = zv * sig
        uw = u * ow[:, c]
        cotw = jnp.concatenate([cotb] * (step // 128), axis=1)
        for t in range(step // 128):
            lsum = lsum + uw[:, t * 128:(t + 1) * 128]
        g_ow[:, c] = jnp.sum(u * cotw, axis=0, keepdims=True)
        dz = cotw * ow[:, c] * (sig * (1.0 + zv * (1.0 - sig)))
        g_tb[:, c] = jnp.sum(dz, axis=0, keepdims=True)
        dzb[:, c] = dz.astype(BF16)
    logits[...] = jnp.sum(lsum.T, axis=0, keepdims=True)

    @pl.loop(0, width // step)
    def _(j):
        c = pl.ds(pl.multiple_of(j * step, step), step)
        dhv = dot(dzb[...], tw[c, :], NT)
        dh[:, c] = dhv
        dy = dhv * x0[:, c].astype(F32)
        g_cb[:, c] = jnp.sum(dy, axis=0, keepdims=True)
        dyb[:, c] = dy.astype(BF16)

    @pl.loop(0, width // step)
    def _(j):
        c = pl.ds(pl.multiple_of(j * step, step), step)
        g_top[c, :] = dot(h[:, c], dzb[...], TN)
        g_cross[c, :] = dot(x0[:, c], dyb[...], TN)

    @pl.loop(0, width // step)
    def _(j):
        c = pl.ds(pl.multiple_of(j * step, step), step)
        dx = dh[:, c] * (y[:, c] + 1.0) + dot(dyb[...], cw[c, :], NT)
        for t in range(step // emb):
            dxhl[j * (step // emb) + t] = split(dx[:, t * emb:(t + 1) * emb])

    sub = lax.broadcasted_iota(I32, (cap, samples), 0)
    for f in range(feats):
        sums = [jnp.zeros((cap, samples), I32)] * groups
        for b in range(bag):
            row = b * feats + f
            code = jnp.broadcast_to(rowcode[row:row + 1, :], (cap, samples)) - sub
            bit = jnp.broadcast_to(rowbit[row:row + 1, :], (cap, samples))
            for w in range(groups):
                sums[w] = sums[w] + jnp.where(code == w * cap, bit, 0)
        for w in range(groups):
            wordst[w, f] = sums[w]

    @pl.loop(0, owners // per)
    def _(g):
        w = g // 2
        total = jnp.zeros((per * cap, 2 * emb), F32)
        for f in range(feats):
            word = wordst[w, f]
            tiles = []
            for i in range(per):
                mask = jnp.left_shift(jnp.int32(15), ((g % 2) * per + i) * 4)
                tiles.append((word & mask).astype(F32).astype(BF16))
            total = total + dot(jnp.concatenate(tiles, axis=0), dxhl[f], NN)
        for i in range(per):
            o = g * per + i
            rows = total[i * cap:(i + 1) * cap]
            slot_grads[o] = (rows[:, :emb] + rows[:, emb:]) * nibble_scale(o)


def local_step(cache, slots, lengths, cot, cw, cb, tw, tb, ow):
    feats, bag, samples = slots.shape
    owners, cap, emb = cache.shape
    width, top = tw.shape
    groups = owners // 8
    vm = pl.BlockSpec(memory_space=pltpu.VMEM)
    out = [
        jax.ShapeDtypeStruct((1, samples), F32),
        jax.ShapeDtypeStruct((width, width), F32),
        jax.ShapeDtypeStruct((width, top), F32),
        jax.ShapeDtypeStruct((1, width), F32),
        jax.ShapeDtypeStruct((1, top), F32),
        jax.ShapeDtypeStruct((1, top), F32),
        jax.ShapeDtypeStruct((owners, cap, emb), F32),
    ]
    keys = feats * bag
    scratch = [
        pltpu.VMEM((groups, feats, samples, cap), I32),
        pltpu.VMEM((groups, feats, cap, samples), I32),
        pltpu.VMEM((samples, keys), I32),
        pltpu.VMEM((samples, keys), I32),
        pltpu.VMEM((keys, samples), I32),
        pltpu.VMEM((keys, samples), I32),
        pltpu.VMEM((feats, samples, 2 * emb), F32),
        pltpu.VMEM((owners * cap, 2 * emb), BF16),
        pltpu.VMEM((samples, width), BF16),
        pltpu.VMEM((samples, width), F32),
        pltpu.VMEM((samples, width), BF16),
        pltpu.VMEM((samples, top), F32),
        pltpu.VMEM((samples, top), BF16),
        pltpu.VMEM((samples, width), BF16),
        pltpu.VMEM((samples, width), F32),
        pltpu.VMEM((feats, samples, 2 * emb), BF16),
    ]
    return pl.pallas_call(
        local_kernel,
        out_shape=out,
        in_specs=[vm] * 9,
        out_specs=[vm] * 7,
        scratch_shapes=scratch,
        compiler_params=pltpu.CompilerParams(vmem_limit_bytes=VMEM_BIG),
        name="local_step",
    )(cache, slots, lengths, cot, cw, cb, tw, tb, ow)

NY = 4


def on_device(table, cross_weight, cross_bias, top_weight, top_bias, out_weight, wanted, slots, lengths, logit_grad):
    emb = table.shape[1]
    cache, served = fetch(wanted[0], table, NY)
    logits, g_cross, g_top, g_cbias, g_tbias, g_out, slot_grads = local_step(
        cache, jnp.transpose(slots, (1, 2, 0)), lengths.T, logit_grad[None], cross_weight, cross_bias[None],
        top_weight, top_bias[None], out_weight[None])
    returned = lax.all_to_all(slot_grads, "shard", split_axis=0, concat_axis=0, tiled=True)
    owner_grad = (
        jnp.zeros(table.shape, jnp.float32).at[served.reshape(-1)].add(returned.reshape(-1, emb))
    )
    table_grad = lax.psum(owner_grad, "dp")
    summed = lax.psum((g_cross, g_top, g_cbias[0], g_tbias[0], g_out[0]), ("dp", "shard"))
    return (logits[0], summed[0], summed[1], summed[2], summed[3], summed[4], table_grad)


def solution(mesh):
    placed = (
        P("shard", None),
        P(),
        P(),
        P(),
        P(),
        P(),
        P(("dp", "shard"), None, None),
        P(("dp", "shard"), None, None),
        P(("dp", "shard"), None),
        P(("dp", "shard")),
    )
    return jax.shard_map(
        on_device,
        mesh=mesh,
        in_specs=placed,
        out_specs=(P(("dp", "shard")), P(), P(), P(), P(), P(), P("shard", None)),
        check_vma=False,
    )
```

```python
import functools
import jax
import jax.numpy as jnp
from jax import lax
from jax.experimental import pallas as pl
from jax.experimental.pallas import tpu as pltpu
from jax.sharding import PartitionSpec as P

VMEM_BIG = 60 * 1024 * 1024
F32, BF16, I32 = jnp.float32, jnp.bfloat16, jnp.int32


def dot(a, b, dims):
    return lax.dot_general(a, b, (dims, ((), ())), preferred_element_type=F32)


NN = ((1,), (0,))
NT = ((1,), (1,))
TN = ((0,), (0,))


def split(x):
    hi = x.astype(BF16)
    lo = (x - hi.astype(F32)).astype(BF16)
    return jnp.concatenate([hi, lo], axis=1)


def nibble_scale(o):
    k = o % 8
    s = jnp.where((k & 1) == 1, F32(2.0**-4), F32(1.0))
    s = s * jnp.where((k & 2) == 2, F32(2.0**-8), F32(1.0))
    return s * jnp.where((k & 4) == 4, F32(2.0**-16), F32(1.0))


def key_codes(slots, lengths, b):
    slot = slots[:, b, :]
    owner = slot >> 7
    code = jnp.where(lengths[...] > b, (slot & 127) + ((owner >> 3) << 7), -1)
    return code, jnp.left_shift(jnp.ones_like(owner), (owner & 7) << 2)


def local_kernel(cache, slots, lengths, cot, cw, cb, tw, tb, ow,
                 logits, dense, small, slot_grads,
                 words, wordst, colcode, colbit, rowcode, rowbit, acc, chl, x0, y, h, z, dzb, dyb, dh, dxhl):
    feats, bag, samples = slots.shape
    owners, cap, emb = cache.shape
    width, top = tw.shape
    groups = words.shape[0]

    for b in range(bag):
        code, bit = key_codes(slots, lengths, b)
        rowcode[pl.ds(b * feats, feats), :] = code
        rowbit[pl.ds(b * feats, feats), :] = bit
    colcode[...] = rowcode[...].T
    colbit[...] = rowbit[...].T

    lane = lax.broadcasted_iota(I32, (samples, cap), 1)
    for f in range(feats):
        sums = [jnp.zeros((samples, cap), I32)] * groups
        for b in range(bag):
            col = b * feats + f
            code = jnp.broadcast_to(colcode[:, col:col + 1], (samples, cap)) - lane
            bit = jnp.broadcast_to(colbit[:, col:col + 1], (samples, cap))
            for w in range(groups):
                sums[w] = sums[w] + jnp.where(code == w * cap, bit, 0)
        for w in range(groups):
            words[w, f] = sums[w]

    for o in range(owners):
        scale = 2.0 ** -(4 * (o % 8))
        chl[pl.ds(o * cap, cap), :] = split(cache[o] * scale)

    per = 4

    @pl.loop(0, owners // per)
    def _(g):
        w = g // 2
        rhs = chl[pl.ds(g * per * cap, per * cap), :]

        @pl.loop(0, feats)
        def _(f):
            word = words[w, f]
            tiles = []
            for i in range(per):
                mask = jnp.left_shift(jnp.int32(15), ((g % 2) * per + i) * 4)
                tiles.append((word & mask).astype(F32).astype(BF16))
            part = dot(jnp.concatenate(tiles, axis=1), rhs, NN)

            @pl.when(g == 0)
            def _():
                acc[f] = part

            @pl.when(g > 0)
            def _():
                acc[f] += part

    for f in range(feats):
        x0[:, f * emb:(f + 1) * emb] = (acc[f, :, :emb] + acc[f, :, emb:]).astype(BF16)

    step = 256

    def put_dense(j, at, val):
        n = step // 8
        for t in range(val.shape[1] // 128):
            dense[pl.ds(j * n, n), at + t] = val[:, t * 128:(t + 1) * 128].reshape(n, 8, 128)

    def put_small(at, row, vec):
        for t in range(step // 128):
            small[pl.ds(at + row + t, 1), :] = vec[:, t * 128:(t + 1) * 128]

    @pl.loop(0, width // step)
    def _(j):
        c = pl.ds(pl.multiple_of(j * step, step), step)
        yv = dot(x0[...], cw[:, c], NN) + cb[:, c]
        y[:, c] = yv
        xf = x0[:, c].astype(F32)
        h[:, c] = (xf * yv + xf).astype(BF16)

    cotb = jnp.broadcast_to(cot[...], (128, samples)).T
    lsum = jnp.zeros((samples, 128), F32)
    for j in range(top // step):
        c = pl.ds(j * step, step)
        zv = dot(h[...], tw[:, c], NN) + tb[:, c]
        sig = jax.nn.sigmoid(zv)
        u = zv * sig
        uw = u * ow[:, c]
        cotw = jnp.concatenate([cotb] * (step // 128), axis=1)
        for t in range(step // 128):
            lsum = lsum + uw[:, t * 128:(t + 1) * 128]
        put_small((width + top) // 128, j * (step // 128), jnp.sum(u * cotw, axis=0, keepdims=True))
        dz = cotw * ow[:, c] * (sig * (1.0 + zv * (1.0 - sig)))
        put_small(width // 128, j * (step // 128), jnp.sum(dz, axis=0, keepdims=True))
        dzb[:, c] = dz.astype(BF16)
    logits[...] = jnp.sum(lsum.T, axis=0, keepdims=True)

    @pl.loop(0, width // step)
    def _(j):
        c = pl.ds(pl.multiple_of(j * step, step), step)
        dhv = dot(dzb[...], tw[c, :], NT)
        dh[:, c] = dhv
        dy = dhv * x0[:, c].astype(F32)
        put_small(0, j * (step // 128), jnp.sum(dy, axis=0, keepdims=True))
        dyb[:, c] = dy.astype(BF16)

    @pl.loop(0, width // step)
    def _(j):
        c = pl.ds(pl.multiple_of(j * step, step), step)
        put_dense(j, width // 128, dot(h[:, c], dzb[...], TN))
        put_dense(j, 0, dot(x0[:, c], dyb[...], TN))

    @pl.loop(0, width // step)
    def _(j):
        c = pl.ds(pl.multiple_of(j * step, step), step)
        dx = dh[:, c] * (y[:, c] + 1.0) + dot(dyb[...], cw[c, :], NT)
        for t in range(step // emb):
            dxhl[j * (step // emb) + t] = split(dx[:, t * emb:(t + 1) * emb])

    sub = lax.broadcasted_iota(I32, (cap, samples), 0)
    for f in range(feats):
        sums = [jnp.zeros((cap, samples), I32)] * groups
        for b in range(bag):
            row = b * feats + f
            code = jnp.broadcast_to(rowcode[row:row + 1, :], (cap, samples)) - sub
            bit = jnp.broadcast_to(rowbit[row:row + 1, :], (cap, samples))
            for w in range(groups):
                sums[w] = sums[w] + jnp.where(code == w * cap, bit, 0)
        for w in range(groups):
            wordst[w, f] = sums[w]

    @pl.loop(0, owners // per)
    def _(g):
        w = g // 2
        total = jnp.zeros((per * cap, 2 * emb), F32)
        for f in range(feats):
            word = wordst[w, f]
            tiles = []
            for i in range(per):
                mask = jnp.left_shift(jnp.int32(15), ((g % 2) * per + i) * 4)
                tiles.append((word & mask).astype(F32).astype(BF16))
            total = total + dot(jnp.concatenate(tiles, axis=0), dxhl[f], NN)
        for i in range(per):
            o = g * per + i
            rows = total[i * cap:(i + 1) * cap]
            slot_grads[o] = (rows[:, :emb] + rows[:, emb:]) * nibble_scale(o)


def local_step(cache, slots, lengths, cot, cw, cb, tw, tb, ow):
    feats, bag, samples = slots.shape
    owners, cap, emb = cache.shape
    width, top = tw.shape
    groups = owners // 8
    vm = pl.BlockSpec(memory_space=pltpu.VMEM)
    out = [
        jax.ShapeDtypeStruct((1, samples), F32),
        jax.ShapeDtypeStruct((width // 8, (width + top) // 128, 8, 128), F32),
        jax.ShapeDtypeStruct(((width + 2 * top) // 128, 128), F32),
        jax.ShapeDtypeStruct((owners, cap, emb), F32),
    ]
    keys = feats * bag
    scratch = [
        pltpu.VMEM((groups, feats, samples, cap), I32),
        pltpu.VMEM((groups, feats, cap, samples), I32),
        pltpu.VMEM((samples, keys), I32),
        pltpu.VMEM((samples, keys), I32),
        pltpu.VMEM((keys, samples), I32),
        pltpu.VMEM((keys, samples), I32),
        pltpu.VMEM((feats, samples, 2 * emb), F32),
        pltpu.VMEM((owners * cap, 2 * emb), BF16),
        pltpu.VMEM((samples, width), BF16),
        pltpu.VMEM((samples, width), F32),
        pltpu.VMEM((samples, width), BF16),
        pltpu.VMEM((samples, top), F32),
        pltpu.VMEM((samples, top), BF16),
        pltpu.VMEM((samples, width), BF16),
        pltpu.VMEM((samples, width), F32),
        pltpu.VMEM((feats, samples, 2 * emb), BF16),
    ]
    return pl.pallas_call(
        local_kernel,
        out_shape=out,
        in_specs=[vm] * 9,
        out_specs=[vm] * 4,
        scratch_shapes=scratch,
        compiler_params=pltpu.CompilerParams(vmem_limit_bytes=VMEM_BIG),
        name="local_step",
    )(cache, slots, lengths, cot, cw, cb, tw, tb, ow)


def peer_of(k, me, ny, nz):
    j = k // ny
    dz = nz // 2 + (j // 2 + j % 2) * (1 - 2 * (j % 2))
    dy = (k + 1) % ny
    z = (me // ny + dz + nz) % nz
    y = (me % ny + dy) % ny
    return z * ny + y


def fetch_kernel(n, ny, wanted, table, cache, ids_in, ids_sm, sendbuf,
                 id_send, id_recv, row_send, row_recv, sm_sem):
    nz = n // ny
    cap = wanted.shape[2]
    me = lax.axis_index("shard")
    barrier = pltpu.get_barrier_semaphore()

    @pl.loop(0, n - 1)
    def _(k):
        pl.semaphore_signal(barrier, inc=1, device_id={"shard": peer_of(k, me, ny, nz)})

    pl.semaphore_wait(barrier, n - 1)

    def id_copy(p):
        return pltpu.make_async_remote_copy(
            src_ref=wanted.at[p], dst_ref=ids_in.at[me], send_sem=id_send.at[p],
            recv_sem=id_recv.at[me], device_id={"shard": p})

    def id_arrival(p):
        return pltpu.make_async_remote_copy(
            src_ref=wanted.at[p], dst_ref=ids_in.at[p], send_sem=id_send.at[p],
            recv_sem=id_recv.at[p], device_id={"shard": p})

    def row_copy(p):
        return pltpu.make_async_remote_copy(
            src_ref=sendbuf.at[p], dst_ref=cache.at[me], send_sem=row_send.at[p],
            recv_sem=row_recv.at[me], device_id={"shard": p})

    def row_arrival(p):
        return pltpu.make_async_remote_copy(
            src_ref=sendbuf.at[p], dst_ref=cache.at[p], send_sem=row_send.at[p],
            recv_sem=row_recv.at[p], device_id={"shard": p})

    @pl.loop(0, n - 1)
    def _(k):
        id_copy(peer_of(k, me, ny, nz)).start()

    ids_in[me] = wanted[me]

    @pl.loop(0, n - 1)
    def _(k):
        id_arrival(peer_of(k, me, ny, nz)).wait_recv()

    to_smem = pltpu.make_async_copy(ids_in, ids_sm, sm_sem)
    to_smem.start()
    to_smem.wait()

    def serve(p, out):
        @pl.loop(0, cap // 16)
        def _(t):
            for i in range(16):
                row = t * 16 + i
                out[p, pl.ds(row, 1), :] = table[pl.ds(ids_sm[p, 0, row], 1), :]

    @pl.loop(0, n - 1)
    def _(k):
        p = peer_of(k, me, ny, nz)
        serve(p, sendbuf)
        row_copy(p).start()

    serve(me, cache)

    @pl.loop(0, n - 1)
    def _(k):
        p = peer_of(k, me, ny, nz)
        row_arrival(p).wait_recv()

    @pl.loop(0, n - 1)
    def _(k):
        p = peer_of(k, me, ny, nz)
        id_copy(p).wait_send()
        row_copy(p).wait_send()


def fetch(wanted, table, ny):
    n, cap = wanted.shape
    emb = table.shape[1]
    vm = pl.BlockSpec(memory_space=pltpu.VMEM)
    cache, served = pl.pallas_call(
        functools.partial(fetch_kernel, n, ny),
        out_shape=[
            jax.ShapeDtypeStruct((n, cap, emb), jnp.float32),
            jax.ShapeDtypeStruct((n, 1, cap), jnp.int32),
        ],
        in_specs=[vm, vm],
        out_specs=[vm, vm],
        scratch_shapes=[
            pltpu.SMEM((n, 1, cap), jnp.int32),
            pltpu.VMEM((n, cap, emb), jnp.float32),
            pltpu.SemaphoreType.DMA((n,)),
            pltpu.SemaphoreType.DMA((n,)),
            pltpu.SemaphoreType.DMA((n,)),
            pltpu.SemaphoreType.DMA((n,)),
            pltpu.SemaphoreType.DMA,
        ],
        compiler_params=pltpu.CompilerParams(
            collective_id=0, has_side_effects=True, vmem_limit_bytes=VMEM_BIG),
        name="fetch_rows",
    )(wanted.reshape(n, 1, cap), table)
    return cache, served


def add_tiles(out, parts, count, chunk):
    chunk = min(chunk, count)

    @pl.loop(0, count // chunk)
    def _(t):
        w = pl.ds(t * chunk, chunk)
        total = parts[0][w]
        for p in parts[1:]:
            total = total + p[w]
        out[w] = total


class Group:
    def __init__(self, size, me, address):
        self.size, self.me, self.address = size, me, address

    def others(self):
        return [(d, (self.me + d) % self.size) for d in range(1, self.size)]


def spread(group, src, dst, send, recv):
    copies = []
    for d, j in group.others():
        cp = pltpu.make_async_remote_copy(
            src_ref=src(j), dst_ref=dst(group.me), send_sem=send.at[d],
            recv_sem=recv.at[group.me], device_id=group.address(j))
        cp.start()
        copies.append(cp)
    return copies


def gather_wait(group, src, dst, send, recv):
    for d, j in group.others():
        pltpu.make_async_remote_copy(
            src_ref=src(j), dst_ref=dst(j), send_sem=send.at[d],
            recv_sem=recv.at[j], device_id=group.address(j)).wait_recv()


def reduce_kernel(nx, ny, nz, slot_grads, served, dense, small,
                  table_out, dense_out, small_out,
                  back, tsum, rt1, rt2, r1, r2, r3, r4, b, c3,
                  s_core, s_x, s_y, s_z, sm1, sm2, sm3,
                  g_send, g_recv, core_send, core_recv, st_send, st_recv, z_send, z_recv, sm_send, sm_recv):
    n = ny * nz
    cap = served.shape[2]
    emb = slot_grads.shape[2]
    rows = tsum.shape[0]
    dp, me = lax.axis_index("dp"), lax.axis_index("shard")
    x, core, z, y = dp // 2, dp % 2, me // ny, me % ny
    gx = Group(nx, x, lambda j: {"dp": j * 2 + core})
    gy = Group(ny, y, lambda j: {"shard": z * ny + j})
    gz = Group(nz, z, lambda j: {"shard": j * ny + y})
    gc = Group(2, core, lambda j: {"dp": x * 2 + j})

    barrier = pltpu.get_barrier_semaphore()

    @pl.loop(0, n - 1)
    def _(k):
        pl.semaphore_signal(barrier, inc=1, device_id={"shard": peer_of(k, me, ny, nz)})

    for grp in (gx, gc):
        for _, j in grp.others():
            pl.semaphore_signal(barrier, inc=1, device_id=grp.address(j))
    pl.semaphore_wait(barrier, n - 1 + nx - 1 + 1)

    pending = []
    tiles = dense.shape[0]
    half = tiles // 2
    quarter = half // 2
    order = [(gx, gy), (gy, gx)]

    mine = lambda h: dense.at[pl.ds(core * half + h * quarter, quarter)]
    theirs = lambda h: dense.at[pl.ds((1 - core) * half + h * quarter, quarter)]
    for h in range(2):
        pending += spread(gc, lambda j: theirs(h), lambda i: r1.at[h], core_send.at[h], core_recv.at[h])
    s_core[core] = small[...]
    pending += spread(gc, lambda j: small, lambda i: s_core.at[i], sm_send.at[0], sm_recv.at[0])

    def grad_copy(p):
        return pltpu.make_async_remote_copy(
            src_ref=slot_grads.at[p], dst_ref=back.at[me], send_sem=g_send.at[p],
            recv_sem=g_recv.at[me], device_id={"shard": p})

    def grad_arrival(p):
        return pltpu.make_async_remote_copy(
            src_ref=slot_grads.at[p], dst_ref=back.at[p], send_sem=g_send.at[p],
            recv_sem=g_recv.at[p], device_id={"shard": p})

    @pl.loop(0, n - 1)
    def _(k):
        grad_copy(peer_of(k, me, ny, nz)).start()

    back[me] = slot_grads[me]

    piece = [quarter // order[h][0].size for h in range(2)]
    sub = [piece[h] // order[h][1].size for h in range(2)]
    unit = sub[0] // nz

    def small_sum(slots, out):
        total = slots[0]
        for i in range(1, slots.shape[0]):
            total = total + slots[i]
        out[...] = total

    for h in range(2):
        grp = order[h][0]
        gather_wait(gc, lambda j: theirs(h), lambda i: r1.at[h], core_send.at[h], core_recv.at[h])
        add_tiles(r1.at[h], [r1.at[h], mine(h)], quarter, 32)
        src = lambda j: r1.at[h, pl.ds(j * piece[h], piece[h])]
        pending += spread(grp, src, lambda i: r2[h].at[i], st_send.at[0, h], st_recv.at[0, h])
    gather_wait(gc, lambda j: small, lambda i: s_core.at[i], sm_send.at[0], sm_recv.at[0])
    small_sum(s_core, sm1)
    s_x[x] = sm1[...]
    pending += spread(gx, lambda j: sm1, lambda i: s_x.at[i], sm_send.at[1], sm_recv.at[1])

    for h in range(2):
        grp, nxt = order[h]
        src = lambda j: r1.at[h, pl.ds(j * piece[h], piece[h])]
        gather_wait(grp, src, lambda i: r2[h].at[i], st_send.at[0, h], st_recv.at[0, h])
        add_tiles(b[h], [src(grp.me)] + [r2[h].at[j] for _, j in grp.others()], piece[h], 24)
        src2 = lambda j: b[h].at[pl.ds(j * sub[h], sub[h])]
        pending += spread(nxt, src2, lambda i: r3[h].at[i], st_send.at[1, h], st_recv.at[1, h])
    gather_wait(gx, lambda j: sm1, lambda i: s_x.at[i], sm_send.at[1], sm_recv.at[1])
    small_sum(s_x, sm2)
    s_y[y] = sm2[...]
    pending += spread(gy, lambda j: sm2, lambda i: s_y.at[i], sm_send.at[2], sm_recv.at[2])

    for h in range(2):
        nxt = order[h][1]
        src2 = lambda j: b[h].at[pl.ds(j * sub[h], sub[h])]
        gather_wait(nxt, src2, lambda i: r3[h].at[i], st_send.at[1, h], st_recv.at[1, h])
        add_tiles(c3.at[h], [src2(nxt.me)] + [r3[h].at[j] for _, j in nxt.others()], sub[h], 24)
        src3 = lambda j: c3.at[h, pl.ds(j * unit, unit)]
        pending += spread(gz, src3, lambda i: r4.at[h, i], z_send.at[0, h], z_recv.at[0, h])
    gather_wait(gy, lambda j: sm2, lambda i: s_y.at[i], sm_send.at[2], sm_recv.at[2])
    small_sum(s_y, sm3)
    s_z[z] = sm3[...]
    pending += spread(gz, lambda j: sm3, lambda i: s_z.at[i], sm_send.at[3], sm_recv.at[3])

    def at1(h, a):
        return core * half + h * quarter + a * piece[h]

    def at2(h, a, bb):
        return at1(h, a) + bb * sub[h]

    def at3(h, zz):
        return at2(h, order[h][0].me, order[h][1].me) + zz * unit

    for h in range(2):
        src3 = lambda j: c3.at[h, pl.ds(j * unit, unit)]
        gather_wait(gz, src3, lambda i: r4.at[h, i], z_send.at[0, h], z_recv.at[0, h])
        here = lambda i: dense_out.at[pl.ds(at3(h, i), unit)]
        add_tiles(here(z), [src3(z)] + [r4.at[h, j] for _, j in gz.others()], unit, unit)
        pending += spread(gz, lambda j: here(z), here, z_send.at[1, h], z_recv.at[1, h])
    gather_wait(gz, lambda j: sm3, lambda i: s_z.at[i], sm_send.at[3], sm_recv.at[3])
    small_sum(s_z, small_out)

    def owner_sum(j):
        zp = (z + nz // 2 - (j // 2 + j % 2) * (1 - 2 * (j % 2)) + nz) % nz
        first = zp * ny

        @pl.loop(0, ny)
        def _(i):
            p = first + i

            @pl.when(p != me)
            def _():
                grad_arrival(p).wait_recv()

        rhs = jnp.concatenate([split(back[first + i]) for i in range(ny)], axis=0)
        ids = jnp.concatenate([served[first + i] for i in range(ny)], axis=1)
        step = 256

        @pl.loop(0, rows // step)
        def _(t):
            at = t * step
            row = lax.broadcasted_iota(I32, (step, ny * cap), 0) + at
            hot = jnp.where(row == ids, F32(1), F32(0)).astype(BF16)
            part = dot(hot, rhs, NN)
            part = part[:, :emb] + part[:, emb:]
            w = pl.ds(pl.multiple_of(at, step), step)
            tsum[w] = jnp.where(j == 0, part, tsum[w] + part)

    @pl.loop(0, nz)
    def _(j):
        owner_sum(j)

    for h in range(2):
        nxt = order[h][1]
        here = lambda i: dense_out.at[pl.ds(at3(h, i), unit)]
        gather_wait(gz, lambda j: here(z), here, z_send.at[1, h], z_recv.at[1, h])
        here2 = lambda i: dense_out.at[pl.ds(at2(h, order[h][0].me, i), sub[h])]
        pending += spread(nxt, lambda j: here2(nxt.me), here2, st_send.at[2, h], st_recv.at[2, h])

    thalf = rows // 2
    tq = thalf // nx
    tw = lambda c: tsum.at[pl.ds(pl.multiple_of(c * thalf, thalf), thalf)]
    pending += spread(gc, lambda j: tw(j), lambda i: rt1, core_send.at[2], core_recv.at[2])

    for h in range(2):
        grp, nxt = order[h]
        here2 = lambda i: dense_out.at[pl.ds(at2(h, grp.me, i), sub[h])]
        gather_wait(nxt, lambda j: here2(nxt.me), here2, st_send.at[2, h], st_recv.at[2, h])
        here1 = lambda i: dense_out.at[pl.ds(at1(h, i), piece[h])]
        pending += spread(grp, lambda j: here1(grp.me), here1, st_send.at[3, h], st_recv.at[3, h])

    gather_wait(gc, lambda j: tw(j), lambda i: rt1, core_send.at[2], core_recv.at[2])
    rt1[...] = rt1[...] + tsum[pl.ds(pl.multiple_of(core * thalf, thalf), thalf)]
    tsrc = lambda j: rt1.at[pl.ds(pl.multiple_of(j * tq, tq), tq)]
    pending += spread(gx, tsrc, lambda i: rt2.at[i], st_send.at[4, 0], st_recv.at[4, 0])

    for h in range(2):
        grp = order[h][0]
        here1 = lambda i: dense_out.at[pl.ds(at1(h, i), piece[h])]
        gather_wait(grp, lambda j: here1(grp.me), here1, st_send.at[3, h], st_recv.at[3, h])
        part = lambda i: dense_out.at[pl.ds(i * half + h * quarter, quarter)]
        pending += spread(gc, lambda j: part(core), part, core_send.at[3 + h], core_recv.at[3 + h])

    gather_wait(gx, tsrc, lambda i: rt2.at[i], st_send.at[4, 0], st_recv.at[4, 0])
    tplace = lambda c, i: table_out.at[pl.ds(pl.multiple_of(c * thalf + i * tq, tq), tq)]
    total = rt1[pl.ds(pl.multiple_of(x * tq, tq), tq)]
    for _, j in gx.others():
        total = total + rt2[j]
    table_out[pl.ds(pl.multiple_of(core * thalf + x * tq, tq), tq)] = total
    there = lambda i: tplace(core, i)
    pending += spread(gx, lambda j: there(x), there, st_send.at[4, 1], st_recv.at[4, 1])
    gather_wait(gx, lambda j: there(x), there, st_send.at[4, 1], st_recv.at[4, 1])
    tside = lambda i: table_out.at[pl.ds(pl.multiple_of(i * thalf, thalf), thalf)]
    pending += spread(gc, lambda j: tside(core), tside, core_send.at[5], core_recv.at[5])

    for h in range(2):
        part = lambda i: dense_out.at[pl.ds(i * half + h * quarter, quarter)]
        gather_wait(gc, lambda j: part(core), part, core_send.at[3 + h], core_recv.at[3 + h])
    gather_wait(gc, lambda j: tside(core), tside, core_send.at[5], core_recv.at[5])

    for cp in pending:
        cp.wait_send()

    @pl.loop(0, n - 1)
    def _(k):
        grad_copy(peer_of(k, me, ny, nz)).wait_send()


def reduce_all(slot_grads, served, dense, small, nx, ny, nz, rows):
    n, cap, emb = slot_grads.shape
    tiles = dense.shape[0]
    quarter = tiles // 4
    vm = pl.BlockSpec(memory_space=pltpu.VMEM)
    t = lambda *lead: pltpu.VMEM((*lead, 8, 128), F32)
    ns = (nx, ny)
    sizes = [(nx, ny), (ny, nx)]
    piece = [quarter // a for a, _ in sizes]
    sub = quarter // (nx * ny)
    sm = small.shape
    top = max(nx, ny)
    dma = lambda *s: pltpu.SemaphoreType.DMA(s)

    def body(*refs):
        ins, outs, rest = refs[:4], refs[4:7], refs[7:]
        back, tsum, rt1, rt2, r1, r2a, r2b, r3a, r3b, r4, ba, bb, c3 = rest[:13]
        reduce_kernel(nx, ny, nz, *ins, *outs, back, tsum, rt1, rt2, r1, (r2a, r2b), (r3a, r3b), r4, (ba, bb), c3, *rest[13:])

    return pl.pallas_call(
        body,
        out_shape=[
            jax.ShapeDtypeStruct((rows, emb), F32),
            jax.ShapeDtypeStruct(dense.shape, F32),
            jax.ShapeDtypeStruct(sm, F32),
        ],
        in_specs=[vm] * 4,
        out_specs=[vm] * 3,
        scratch_shapes=[
            pltpu.VMEM((n, cap, emb), F32),
            pltpu.VMEM((rows, emb), F32),
            pltpu.VMEM((rows // 2, emb), F32),
            pltpu.VMEM((nx, rows // 2 // nx, emb), F32),
            t(2, quarter),
            t(nx, piece[0]), t(ny, piece[1]),
            t(ny, sub), t(nx, sub),
            t(2, nz, sub // nz),
            t(piece[0]), t(piece[1]),
            t(2, sub),
            pltpu.VMEM((2, *sm), F32), pltpu.VMEM((nx, *sm), F32), pltpu.VMEM((ny, *sm), F32), pltpu.VMEM((nz, *sm), F32),
            pltpu.VMEM(sm, F32), pltpu.VMEM(sm, F32), pltpu.VMEM(sm, F32),
            dma(n), dma(n),
            dma(6, 2), dma(6, 2),
            dma(5, 2, top), dma(5, 2, top),
            dma(2, 2, nz), dma(2, 2, nz),
            dma(4, max(nz, top)), dma(4, max(nz, top)),
        ],
        compiler_params=pltpu.CompilerParams(
            collective_id=1, has_side_effects=True, vmem_limit_bytes=VMEM_BIG),
        name="reduce_all",
    )(slot_grads, served, dense, small)


NX, NY = 4, 4


def on_device(table, cross_weight, cross_bias, top_weight, top_bias, out_weight, wanted, slots, lengths, logit_grad):
    width, top = top_weight.shape
    n = wanted.shape[1]
    cache, served = fetch(wanted[0], table, NY)
    logits, dense, small, slot_grads = local_step(
        cache, jnp.transpose(slots, (1, 2, 0)), lengths.T, logit_grad[None], cross_weight, cross_bias[None],
        top_weight, top_bias[None], out_weight[None])
    table_grad, summed, vecs = reduce_all(
        slot_grads, served, dense.reshape(-1, 8, 128), small, NX, NY, n // NY, table.shape[0])
    tiles = summed.reshape(dense.shape)
    cut = width // 128
    g_cross = jnp.transpose(tiles[:, :cut], (0, 2, 1, 3)).reshape(width, width)
    g_top = jnp.transpose(tiles[:, cut:], (0, 2, 1, 3)).reshape(width, top)
    vec = vecs.reshape(-1)
    return (logits[0], g_cross, g_top, vec[:width], vec[width:width + top], vec[width + top:], table_grad)


def solution(mesh):
    placed = (
        P("shard", None),
        P(),
        P(),
        P(),
        P(),
        P(),
        P(("dp", "shard"), None, None),
        P(("dp", "shard"), None, None),
        P(("dp", "shard"), None),
        P(("dp", "shard")),
    )
    return jax.shard_map(
        on_device,
        mesh=mesh,
        in_specs=placed,
        out_specs=(P(("dp", "shard")), P(), P(), P(), P(), P(), P("shard", None)),
        check_vma=False,
    )
```

```python
import functools

import jax
import jax.numpy as jnp
from jax import lax
from jax.experimental import pallas as pl
from jax.experimental.pallas import tpu as pltpu
from jax.sharding import PartitionSpec as P

F32, BF16, I32 = jnp.float32, jnp.bfloat16, jnp.int32
VMEM_LIMIT = 60 * 1024 * 1024
NX, NY = 4, 4
NN = ((1,), (0,))
NT = ((1,), (1,))
TN = ((0,), (0,))


def dot(a, b, dims):
    return lax.dot_general(a, b, (dims, ((), ())), preferred_element_type=F32)


def split(x):
    hi = x.astype(BF16)
    lo = (x - hi.astype(F32)).astype(BF16)
    return jnp.concatenate([hi, lo], axis=1)


def nibble_mask(o):
    return jnp.left_shift(jnp.int32(15), (o % 8) * 4)


def nibble_scale(o):
    k = o % 8
    s = jnp.where((k & 1) == 1, F32(2.0**-4), F32(1.0))
    s = s * jnp.where((k & 2) == 2, F32(2.0**-8), F32(1.0))
    return s * jnp.where((k & 4) == 4, F32(2.0**-16), F32(1.0))


def key_codes(slots, lengths, rowcode, rowbit):
    feats, bag, samples = slots.shape
    for b in range(bag):
        slot = slots[:, b, :]
        owner = slot >> 7
        rowcode[pl.ds(b * feats, feats), :] = jnp.where(
            lengths[...] > b, (slot & 127) + ((owner >> 3) << 7), -1)
        rowbit[pl.ds(b * feats, feats), :] = jnp.left_shift(jnp.ones_like(owner), (owner & 7) << 2)


def count_words(words, feats, bag, code_of, bit_of, place):
    groups, cap = words.shape[0], 128
    for f in range(feats):
        sums = [jnp.zeros(place.shape, I32)] * groups
        for b in range(bag):
            key = b * feats + f
            code = jnp.broadcast_to(code_of(key), place.shape) - place
            bit = jnp.broadcast_to(bit_of(key), place.shape)
            for w in range(groups):
                sums[w] = sums[w] + jnp.where(code == w * cap, bit, 0)
        for w in range(groups):
            words[w, f] = sums[w]


def counts(word, o):
    return (word & nibble_mask(o)).astype(F32).astype(BF16)


class Group:
    def __init__(self, size, me, address):
        self.size, self.me, self.address = size, me, address

    def others(self):
        return [(d, (self.me + d) % self.size) for d in range(1, self.size)]


def plane_step(j, nz):
    return nz // 2 + (j // 2 + j % 2) * (1 - 2 * (j % 2))


def peer_of(k, me, ny, nz):
    z = (me // ny + plane_step(k // ny, nz)) % nz
    y = (me % ny + (k + 1) % ny) % ny
    return z * ny + y


def plane_from(j, z, nz):
    return (z - plane_step(j, nz) + 2 * nz) % nz


def remote(src, dst, send, recv, to):
    return pltpu.make_async_remote_copy(
        src_ref=src, dst_ref=dst, send_sem=send, recv_sem=recv, device_id=to)


def spread(group, src, dst, send, recv):
    copies = []
    for d, j in group.others():
        cp = remote(src(j), dst(group.me), send.at[d], recv.at[group.me], group.address(j))
        cp.start()
        copies.append(cp)
    return copies


def arrived(group, src, dst, send, recv):
    for d, j in group.others():
        remote(src(j), dst(j), send.at[d], recv.at[j], group.address(j)).wait_recv()


def fetch_kernel(n, ny, wanted, table, slots, lengths, x0, ids_in,
                 ids_sm, sendbuf, cache, words, rowcode, rowbit, colcode, colbit, acc,
                 id_send, id_recv, row_send, row_recv, sm_sem):
    nz = n // ny
    cap, emb = cache.shape[1:]
    feats, bag, samples = slots.shape
    me = lax.axis_index("shard")
    z = me // ny
    barrier = pltpu.get_barrier_semaphore()

    @pl.loop(0, n - 1)
    def _(k):
        pl.semaphore_signal(barrier, inc=1, device_id={"shard": peer_of(k, me, ny, nz)})

    pl.semaphore_wait(barrier, n - 1)

    def id_copy(p, slot):
        return remote(wanted.at[p], ids_in.at[slot], id_send.at[p], id_recv.at[slot], {"shard": p})

    def row_copy(p, slot):
        return remote(sendbuf.at[p], cache.at[slot], row_send.at[p], row_recv.at[slot], {"shard": p})

    @pl.loop(0, n - 1)
    def _(k):
        id_copy(peer_of(k, me, ny, nz), me).start()

    ids_in[me] = wanted[me]
    key_codes(slots, lengths, rowcode, rowbit)
    colcode[...] = rowcode[...].T
    colbit[...] = rowbit[...].T

    @pl.loop(0, n - 1)
    def _(k):
        p = peer_of(k, me, ny, nz)
        id_copy(p, p).wait_recv()

    to_smem = pltpu.make_async_copy(ids_in, ids_sm, sm_sem)
    to_smem.start()
    to_smem.wait()

    def serve(p, out):
        @pl.loop(0, cap // 16)
        def _(t):
            for i in range(16):
                row = t * 16 + i
                out[p, pl.ds(row, 1), :] = table[pl.ds(ids_sm[p, 0, row], 1), :]

    @pl.loop(0, n - 1)
    def _(k):
        p = peer_of(k, me, ny, nz)
        serve(p, sendbuf)
        row_copy(p, me).start()

    serve(me, cache)

    count_words(
        words, feats, bag, lambda key: colcode[:, key:key + 1], lambda key: colbit[:, key:key + 1],
        lax.broadcasted_iota(I32, (samples, cap), 1))

    @pl.loop(0, feats)
    def _(f):
        acc[f] = jnp.zeros(acc.shape[1:], F32)

    @pl.loop(0, nz)
    def _(j):
        first = plane_from(j, z, nz) * ny

        @pl.loop(0, ny)
        def _(i):
            p = first + i

            @pl.when(p != me)
            def _():
                row_copy(p, p).wait_recv()

        rhs = jnp.concatenate(
            [split(cache[first + i] * nibble_scale(first + i)) for i in range(ny)], axis=0)

        @pl.loop(0, feats)
        def _(f):
            word = words[first // 8, f]
            lhs = jnp.concatenate([counts(word, first + i) for i in range(ny)], axis=1)
            acc[f] = acc[f] + dot(lhs, rhs, NN)

    for f in range(feats):
        x0[:, f * emb:(f + 1) * emb] = (acc[f, :, :emb] + acc[f, :, emb:]).astype(BF16)

    @pl.loop(0, n - 1)
    def _(k):
        p = peer_of(k, me, ny, nz)
        id_copy(p, me).wait_send()
        row_copy(p, me).wait_send()


def fetch(wanted, table, slots, lengths, ny):
    n, cap = wanted.shape
    emb = table.shape[1]
    feats, bag, samples = slots.shape
    keys = feats * bag
    vm = pl.BlockSpec(memory_space=pltpu.VMEM)
    dma = pltpu.SemaphoreType.DMA
    return pl.pallas_call(
        functools.partial(fetch_kernel, n, ny),
        out_shape=[
            jax.ShapeDtypeStruct((samples, feats * emb), BF16),
            jax.ShapeDtypeStruct((n, 1, cap), I32),
        ],
        in_specs=[vm] * 4,
        out_specs=[vm] * 2,
        scratch_shapes=[
            pltpu.SMEM((n, 1, cap), I32),
            pltpu.VMEM((n, cap, emb), F32),
            pltpu.VMEM((n, cap, emb), F32),
            pltpu.VMEM((pl.cdiv(n, 8), feats, samples, cap), I32),
            pltpu.VMEM((keys, samples), I32),
            pltpu.VMEM((keys, samples), I32),
            pltpu.VMEM((samples, keys), I32),
            pltpu.VMEM((samples, keys), I32),
            pltpu.VMEM((feats, samples, 2 * emb), F32),
            dma((n,)), dma((n,)), dma((n,)), dma((n,)), dma,
        ],
        compiler_params=pltpu.CompilerParams(
            collective_id=0, has_side_effects=True, vmem_limit_bytes=VMEM_LIMIT),
        name="fetch_pool",
    )(wanted.reshape(n, 1, cap), table, slots, lengths)


def add_refs(out, parts, chunk):
    count = out.shape[0]
    chunk = min(chunk, count)

    @pl.loop(0, count // chunk)
    def _(t):
        w = pl.ds(t * chunk, chunk)
        total = parts[0][w]
        for p in parts[1:]:
            total = total + p[w]
        out[w] = total


class Stream:
    def __init__(self, local, out, h, core, first, second, gz, bufs, sems):
        self.local, self.out, self.h = local, out, h
        self.core, self.first, self.second, self.gz = core, first, second, gz
        self.r1, self.r2, self.b, self.r3, self.c, self.r4 = bufs
        self.sems = sems
        self.quarter = local.shape[0] // 4
        self.piece = self.quarter // first.size
        self.unit = self.piece // second.size
        self.pending = []

    def pair(self, k):
        return self.sems[0].at[k], self.sems[1].at[k]

    def go(self, group, src, dst, k):
        self.pending += spread(group, src, dst, *self.pair(k))

    def come(self, group, src, dst, k):
        arrived(group, src, dst, *self.pair(k))

    def half(self, ref, c):
        return ref.at[pl.ds((2 * c + self.h) * self.quarter, self.quarter)]

    def core_args(self):
        return self.core, lambda j: self.half(self.local, j), lambda i: self.r1, 0

    def first_args(self):
        return self.first, lambda j: self.r1.at[pl.ds(j * self.piece, self.piece)], lambda i: self.r2.at[i], 1

    def second_args(self):
        return self.second, lambda j: self.b.at[pl.ds(j * self.unit, self.unit)], lambda i: self.r3.at[i], 2

    def z_args(self):
        return self.gz, lambda j: self.c.at[:, j], lambda i: self.r4.at[i], 3

    def at(self, a=None, bb=None):
        at = (2 * self.core.me + self.h) * self.quarter
        if a is not None:
            at = at + a * self.piece
        if bb is not None:
            at = at + bb * self.unit
        return at

    def zback_args(self):
        here = lambda i: self.out.at[pl.ds(self.at(self.first.me, self.second.me), self.unit), i]
        return self.gz, lambda j: here(self.gz.me), here, 4

    def second_back_args(self):
        here = lambda i: self.out.at[pl.ds(self.at(self.first.me, i), self.unit)]
        return self.second, lambda j: here(self.second.me), here, 5

    def first_back_args(self):
        here = lambda i: self.out.at[pl.ds(self.at(i), self.piece)]
        return self.first, lambda j: here(self.first.me), here, 6

    def core_back_args(self):
        here = lambda i: self.half(self.out, i)
        return self.core, lambda j: here(self.core.me), here, 7

    def step(self, k):
        args = (self.core_args, self.first_args, self.second_args, self.z_args,
                self.zback_args, self.second_back_args, self.first_back_args, self.core_back_args)
        if k >= 0:
            group, src, dst, i = args[k]()
            self.come(group, src, dst, i)
            if k == 0:
                add_refs(self.r1, [self.r1, self.half(self.local, group.me)], 4)
            elif k < 4:
                out = (None, self.b, self.c, None)[k]
                if k == 3:
                    out = self.out.at[pl.ds(self.at(self.first.me, self.second.me), self.unit), self.gz.me]
                add_refs(out, [src(group.me)] + [dst(j) for _, j in group.others()], 2)
        if k + 1 < len(args):
            self.go(*args[k + 1]())


def dense_kernel(nx, ny, nz, x0, slots, lengths, cot, cw, cb, tw, tb, ow, served,
                 logits, table_out, cross_out, top_out, small_out,
                 g_cross, g_top, small, slot_grads, back, tsum, rt1, rt2,
                 words, rowcode, rowbit, y, h, dzb, dyb, dh, dxhl, bufs, sm_bufs, sems):
    n = ny * nz
    cap, emb = back.shape[1:]
    rows = tsum.shape[0]
    feats, bag, samples = slots.shape
    width, top = tw.shape
    dp, me = lax.axis_index("dp"), lax.axis_index("shard")
    x, core, z, yy = dp // 2, dp % 2, me // ny, me % ny
    gx = Group(nx, x, lambda j: {"dp": j * 2 + core})
    gy = Group(ny, yy, lambda j: {"shard": z * ny + j})
    gz = Group(nz, z, lambda j: {"shard": j * ny + yy})
    gc = Group(2, core, lambda j: {"dp": x * 2 + j})
    g_send, g_recv, t_send, t_recv, sm_send, sm_recv, d_send, d_recv = sems

    barrier = pltpu.get_barrier_semaphore()

    @pl.loop(0, n - 1)
    def _(k):
        pl.semaphore_signal(barrier, inc=1, device_id={"shard": peer_of(k, me, ny, nz)})

    for grp in (gx, gc):
        for _, j in grp.others():
            pl.semaphore_signal(barrier, inc=1, device_id=grp.address(j))

    streams = []
    for a, (local, out) in enumerate(((g_top, top_out), (g_cross, cross_out))):
        for hh in range(2):
            first, second = ((gx, gy), (gy, gx))[hh]
            s = 2 * a + hh
            streams.append(Stream(local, out, hh, gc, first, second, gz, bufs[6 * s:6 * s + 6],
                                  (d_send.at[s], d_recv.at[s])))
    tops, crosses = streams[:2], streams[2:]

    step = min(256, width)
    lanes = step // 128

    def put_small(at, vec):
        for t in range(lanes):
            small[pl.ds(at + t, 1), :] = vec[:, t * 128:(t + 1) * 128]

    def put_dense(out, j, val):
        per = val.shape[1] // 128
        deep = nz // per
        count = step // 8 // deep
        for t in range(per):
            v = val[:, t * 128:(t + 1) * 128].reshape(count, deep, 8, 128)
            for i in range(deep):
                out[pl.ds(j * count, count), i * per + t] = v[:, i]

    @pl.loop(0, width // step)
    def _(j):
        c = pl.ds(pl.multiple_of(j * step, step), step)
        yv = dot(x0[...], cw[:, c], NN) + cb[:, c]
        y[:, c] = yv
        xf = x0[:, c].astype(F32)
        h[:, c] = (xf * yv + xf).astype(BF16)

    cotb = jnp.broadcast_to(cot[...], (128, samples)).T
    lsum = jnp.zeros((samples, 128), F32)
    tstep = min(256, top)
    for j in range(top // tstep):
        c = pl.ds(j * tstep, tstep)
        zv = dot(h[...], tw[:, c], NN) + tb[:, c]
        sig = jax.nn.sigmoid(zv)
        u = zv * sig
        uw = u * ow[:, c]
        cotw = jnp.concatenate([cotb] * (tstep // 128), axis=1)
        for t in range(tstep // 128):
            lsum = lsum + uw[:, t * 128:(t + 1) * 128]
        gow = jnp.sum(u * cotw, axis=0, keepdims=True)
        dz = cotw * ow[:, c] * (sig * (1.0 + zv * (1.0 - sig)))
        gtb = jnp.sum(dz, axis=0, keepdims=True)
        for t in range(tstep // 128):
            at = width // 128 + j * (tstep // 128) + t
            small[pl.ds(at, 1), :] = gtb[:, t * 128:(t + 1) * 128]
            small[pl.ds(at + top // 128, 1), :] = gow[:, t * 128:(t + 1) * 128]
        dzb[:, c] = dz.astype(BF16)
    logits[...] = jnp.sum(lsum.T, axis=0, keepdims=True)

    @pl.loop(0, width // step)
    def _(j):
        c = pl.ds(pl.multiple_of(j * step, step), step)
        put_dense(g_top, j, dot(h[:, c], dzb[...], TN))

    pl.semaphore_wait(barrier, n - 1 + nx - 1 + 1)
    for s in tops:
        s.step(-1)

    @pl.loop(0, width // step)
    def _(j):
        c = pl.ds(pl.multiple_of(j * step, step), step)
        dhv = dot(dzb[...], tw[c, :], NT)
        dh[:, c] = dhv
        dy = dhv * x0[:, c].astype(F32)
        put_small(j * lanes, jnp.sum(dy, axis=0, keepdims=True))
        dyb[:, c] = dy.astype(BF16)

    @pl.loop(0, width // step)
    def _(j):
        c = pl.ds(pl.multiple_of(j * step, step), step)
        put_dense(g_cross, j, dot(x0[:, c], dyb[...], TN))

    for s in crosses:
        s.step(-1)
    pending = []
    s_core, s_x, s_y, s_z, sm1, sm2, sm3 = sm_bufs

    def small_go(k, grp, src, slots_):
        slots_[grp.me] = src[...]
        args = (grp, lambda j: src, lambda i: slots_.at[i], sm_send.at[k], sm_recv.at[k])
        pending.extend(spread(*args))
        return args

    def small_come(args, slots_, out):
        arrived(*args)
        total = slots_[0]
        for i in range(1, slots_.shape[0]):
            total = total + slots_[i]
        out[...] = total

    sm_args = small_go(0, gc, small, s_core)

    @pl.loop(0, width // step)
    def _(j):
        c = pl.ds(pl.multiple_of(j * step, step), step)
        dx = dh[:, c] * (y[:, c] + 1.0) + dot(dyb[...], cw[c, :], NT)
        for t in range(step // emb):
            dxhl[j * (step // emb) + t] = split(dx[:, t * emb:(t + 1) * emb])

    for s in tops:
        s.step(0)
    key_codes(slots, lengths, rowcode, rowbit)
    count_words(
        words, feats, bag, lambda key: rowcode[key:key + 1, :], lambda key: rowbit[key:key + 1, :],
        lax.broadcasted_iota(I32, (cap, samples), 0))
    for s in crosses:
        s.step(0)
    small_come(sm_args, s_core, sm1)
    sm_args = small_go(1, gx, sm1, s_x)

    def grad_copy(p, slot):
        return remote(slot_grads.at[p], back.at[slot], g_send.at[p], g_recv.at[slot], {"shard": p})

    def slot_plane(j):
        first = ((z + plane_step(j, nz)) % nz) * ny
        total = jnp.zeros((ny * cap, 2 * emb), F32)
        for f in range(feats):
            word = words[first // 8, f]
            lhs = jnp.concatenate([counts(word, first + i) for i in range(ny)], axis=0)
            total = total + dot(lhs, dxhl[f], NN)
        for i in range(ny):
            part = total[i * cap:(i + 1) * cap]
            slot_grads[first + i] = (part[:, :emb] + part[:, emb:]) * nibble_scale(first + i)

        @pl.loop(0, ny)
        def _(i):
            p = first + (yy + i + 1) % ny

            @pl.when(p != me)
            def _():
                grad_copy(p, me).start()

    @pl.loop(0, nz // 2)
    def _(j):
        slot_plane(j)

    for s in tops:
        s.step(1)

    @pl.loop(nz // 2, nz)
    def _(j):
        slot_plane(j)

    back[me] = slot_grads[me]

    for s in crosses:
        s.step(1)
    small_come(sm_args, s_x, sm2)
    sm_args = small_go(2, gy, sm2, s_y)
    for s in tops:
        s.step(2)
    for s in crosses:
        s.step(2)
    small_come(sm_args, s_y, sm3)
    sm_args = small_go(3, gz, sm3, s_z)
    for s in tops:
        s.step(3)
    for s in crosses:
        s.step(3)
    for s in tops:
        s.step(4)
    for s in crosses:
        s.step(4)
    small_come(sm_args, s_z, small_out)

    def owner_plane(j):
        first = plane_from(j, z, nz) * ny

        @pl.loop(0, ny)
        def _(i):
            p = first + i

            @pl.when(p != me)
            def _():
                grad_copy(p, p).wait_recv()

        rhs = jnp.concatenate([split(back[first + i]) for i in range(ny)], axis=0)
        ids = jnp.concatenate([served[first + i] for i in range(ny)], axis=1)
        mstep = min(512, rows)

        @pl.loop(0, rows // mstep)
        def _(t):
            at = t * mstep
            row = lax.broadcasted_iota(I32, (mstep, ny * cap), 0) + at
            hot = jnp.where(row == ids, F32(1), F32(0)).astype(BF16)
            part = dot(hot, rhs, NN)
            part = part[:, :emb] + part[:, emb:]
            w = pl.ds(pl.multiple_of(at, mstep), mstep)
            tsum[w] = jnp.where(j == 0, part, tsum[w] + part)

    @pl.loop(0, nz // 2)
    def _(j):
        owner_plane(j)

    for s in tops:
        s.step(5)
    for s in crosses:
        s.step(5)

    @pl.loop(nz // 2, nz)
    def _(j):
        owner_plane(j)

    thalf = rows // 2
    tq = thalf // nx
    rows_at = lambda ref, at, size: ref.at[pl.ds(pl.multiple_of(at, size), size)]
    tside = lambda ref, i: rows_at(ref, i * thalf, thalf)
    tpart = lambda ref, i: rows_at(ref, i * tq, tq)
    sem = lambda k: (t_send.at[k], t_recv.at[k])
    tc = (gc, lambda j: tside(tsum, j), lambda i: rt1, *sem(0))
    pending += spread(*tc)
    for s in tops:
        s.step(6)
    arrived(*tc)
    rt1[...] = rt1[...] + tside(tsum, core)[...]
    tx = (gx, lambda j: tpart(rt1, j), lambda i: rt2.at[i], *sem(1))
    pending += spread(*tx)
    for s in crosses:
        s.step(6)
    arrived(*tx)
    mine = tpart(tside(table_out, core), x)
    total = tpart(rt1, x)[...]
    for _, j in gx.others():
        total = total + rt2[j]
    mine[...] = total
    there = lambda i: rows_at(table_out, core * thalf + i * tq, tq)
    tb_ = (gx, lambda j: there(x), there, *sem(2))
    pending += spread(*tb_)
    arrived(*tb_)
    tcb = (gc, lambda j: tside(table_out, core), lambda i: tside(table_out, i), *sem(3))
    pending += spread(*tcb)
    for s in streams:
        s.step(7)
    arrived(*tcb)

    for cp in pending + [cp for s in streams for cp in s.pending]:
        cp.wait_send()

    @pl.loop(0, n - 1)
    def _(k):
        grad_copy(peer_of(k, me, ny, nz), me).wait_send()


def dense_and_reduce(x0, slots, lengths, cot, cw, cb, tw, tb, ow, served, nx, ny, rows):
    samples, width = x0.shape
    top = tw.shape[1]
    feats, bag, _ = slots.shape
    n, _, cap = served.shape
    emb = width // feats
    nz = n // ny
    keys = feats * bag
    vm = pl.BlockSpec(memory_space=pltpu.VMEM)
    v = pltpu.VMEM
    dma = lambda *s: pltpu.SemaphoreType.DMA(s)
    tiles = lambda *lead: (*lead, 8, 128)
    r_cross = width // 8 * (width // 128) // nz
    r_top = width // 8 * (top // 128) // nz
    sm = ((width + 2 * top) // 128, 128)
    most = max(nx, ny, nz)

    bufs = []
    for r in (r_top, r_cross):
        for a, b in ((nx, ny), (ny, nx)):
            q = r // 4
            p = q // a
            u = p // b
            bufs += [v(tiles(q, nz), F32), v(tiles(a, p, nz), F32), v(tiles(p, nz), F32),
                     v(tiles(b, u, nz), F32), v(tiles(u, nz), F32), v(tiles(nz, u), F32)]
    sm_bufs = [v((k, *sm), F32) for k in (2, nx, ny, nz)] + [v(sm, F32)] * 3
    sems = [dma(n), dma(n), dma(4, most), dma(4, most), dma(4, most), dma(4, most), dma(4, 8, most), dma(4, 8, most)]
    own = [
        v(tiles(r_cross, nz), F32), v(tiles(r_top, nz), F32), v(sm, F32),
        v((n, cap, emb), F32), v((n, cap, emb), F32), v((rows, emb), F32),
        v((rows // 2, emb), F32), v((nx, rows // 2 // nx, emb), F32),
        v((pl.cdiv(n, 8), feats, cap, samples), I32), v((keys, samples), I32), v((keys, samples), I32),
        v((samples, width), F32), v((samples, width), BF16), v((samples, top), BF16), v((samples, width), BF16),
        v((samples, width), F32), v((feats, samples, 2 * emb), BF16),
    ]

    def body(*refs):
        head, rest = refs[:15 + len(own)], refs[15 + len(own):]
        dense_kernel(nx, ny, nz, *head, rest[:24], rest[24:31], rest[31:])

    return pl.pallas_call(
        body,
        out_shape=[
            jax.ShapeDtypeStruct((1, samples), F32),
            jax.ShapeDtypeStruct((rows, emb), F32),
            jax.ShapeDtypeStruct(tiles(r_cross, nz), F32),
            jax.ShapeDtypeStruct(tiles(r_top, nz), F32),
            jax.ShapeDtypeStruct(sm, F32),
        ],
        in_specs=[vm] * 10,
        out_specs=[vm] * 5,
        scratch_shapes=own + bufs + sm_bufs + sems,
        compiler_params=pltpu.CompilerParams(
            collective_id=1, has_side_effects=True, vmem_limit_bytes=VMEM_LIMIT),
        name="dense_reduce",
    )(x0, slots, lengths, cot, cw, cb, tw, tb, ow, served)


def from_tiles(tiles, rows, columns):
    return jnp.transpose(tiles.reshape(rows // 8, columns // 128, 8, 128), (0, 2, 1, 3)).reshape(rows, columns)


def on_device(table, cross_weight, cross_bias, top_weight, top_bias, out_weight, wanted, slots, lengths, logit_grad,
              nx=NX, ny=NY):
    width, top = top_weight.shape
    keys, live = jnp.transpose(slots, (1, 2, 0)), lengths.T
    x0, served = fetch(wanted[0], table, keys, live, ny)
    logits, table_grad, cross, tops, vecs = dense_and_reduce(
        x0, keys, live, logit_grad[None], cross_weight, cross_bias[None], top_weight, top_bias[None], out_weight[None],
        served, nx, ny, table.shape[0])
    vec = vecs.reshape(-1)
    return (logits[0], from_tiles(cross, width, width), from_tiles(tops, width, top),
            vec[:width], vec[width:width + top], vec[width + top:], table_grad)


def solution(mesh):
    placed = (
        P("shard", None),
        P(),
        P(),
        P(),
        P(),
        P(),
        P(("dp", "shard"), None, None),
        P(("dp", "shard"), None, None),
        P(("dp", "shard"), None),
        P(("dp", "shard")),
    )
    return jax.shard_map(
        on_device,
        mesh=mesh,
        in_specs=placed,
        out_specs=(P(("dp", "shard")), P(), P(), P(), P(), P(), P("shard", None)),
        check_vma=False,
    )
```

```python
import functools
import math

import jax
import jax.numpy as jnp
from jax import lax
from jax.experimental import pallas as pl
from jax.experimental.pallas import tpu as pltpu
from jax.sharding import PartitionSpec as P

F32, BF16, I32 = jnp.float32, jnp.bfloat16, jnp.int32
VMEM_LIMIT = 60 * 1024 * 1024
NX, NY = 4, 4
NN = ((1,), (0,))
NT = ((1,), (1,))
TN = ((0,), (0,))


def dot(a, b, dims):
    return lax.dot_general(a, b, (dims, ((), ())), preferred_element_type=F32)


def split(x):
    hi = x.astype(BF16)
    lo = (x - hi.astype(F32)).astype(BF16)
    return jnp.concatenate([hi, lo], axis=1)


def nibble_mask(o):
    return jnp.left_shift(jnp.int32(15), (o % 8) * 4)


def nibble_scale(o):
    k = o % 8
    s = jnp.where((k & 1) == 1, F32(2.0**-4), F32(1.0))
    s = s * jnp.where((k & 2) == 2, F32(2.0**-8), F32(1.0))
    return s * jnp.where((k & 4) == 4, F32(2.0**-16), F32(1.0))


def key_codes(slots, lengths, rowcode, rowbit):
    feats, bag, samples = slots.shape
    for b in range(bag):
        slot = slots[:, b, :]
        owner = slot >> 7
        rowcode[pl.ds(b * feats, feats), :] = jnp.where(
            lengths[...] > b, (slot & 127) + ((owner >> 3) << 7), -1)
        rowbit[pl.ds(b * feats, feats), :] = jnp.left_shift(jnp.ones_like(owner), (owner & 7) << 2)


def count_words(words, feats, bag, code_of, bit_of, place):
    groups, cap = words.shape[0], 128
    for f in range(feats):
        sums = [jnp.zeros(place.shape, I32)] * groups
        for b in range(bag):
            key = b * feats + f
            code = jnp.broadcast_to(code_of(key), place.shape) - place
            bit = jnp.broadcast_to(bit_of(key), place.shape)
            for w in range(groups):
                sums[w] = sums[w] + jnp.where(code == w * cap, bit, 0)
        for w in range(groups):
            words[w, f] = sums[w]


def counts(word, o):
    return (word & nibble_mask(o)).astype(F32).astype(BF16)


class Group:
    def __init__(self, size, me, address):
        self.size, self.me, self.address = size, me, address

    def others(self):
        return [(d, (self.me + d) % self.size) for d in range(1, self.size)]


def plane_step(j, nz):
    return ((j + 1) // 2 * (2 * (j % 2) - 1) + nz) % nz


def far_step(j, nz):
    return nz // 2 + (j // 2 + j % 2) * (1 - 2 * (j % 2))


def peer_of(k, me, ny, nz):
    z = (me // ny + plane_step((k + 1) // ny, nz)) % nz
    y = (me % ny + (k + 1) % ny) % ny
    return z * ny + y


def plane_from(step, z, nz):
    return (z - step + 2 * nz) % nz


def remote(src, dst, send, recv, to):
    return pltpu.make_async_remote_copy(
        src_ref=src, dst_ref=dst, send_sem=send, recv_sem=recv, device_id=to)


def spread(group, src, dst, send, recv):
    copies = []
    for d, j in group.others():
        cp = remote(src(j), dst(group.me), send.at[d], recv.at[group.me], group.address(j))
        cp.start()
        copies.append(cp)
    return copies


def arrived(group, src, dst, send, recv):
    for d, j in group.others():
        remote(src(j), dst(j), send.at[d], recv.at[j], group.address(j)).wait_recv()


def fetch_kernel(n, ny, wanted, table, slots, lengths, x0, ids_in, words_out,
                 ids_sm, sendbuf, cache, words, wordst, rowcode, rowbit, colcode, colbit, acc,
                 id_send, id_recv, row_send, row_recv, sm_sem, words_sem):
    nz = n // ny
    cap, emb = cache.shape[1:]
    feats, bag, samples = slots.shape
    me = lax.axis_index("shard")
    z = me // ny
    barrier = pltpu.get_barrier_semaphore()

    @pl.loop(0, n - 1)
    def _(k):
        pl.semaphore_signal(barrier, inc=1, device_id={"shard": peer_of(k, me, ny, nz)})

    pl.semaphore_wait(barrier, n - 1)

    def id_copy(p, slot):
        return remote(wanted.at[p], ids_in.at[slot], id_send.at[p], id_recv.at[slot], {"shard": p})

    def row_copy(p, slot):
        return remote(sendbuf.at[p], cache.at[slot], row_send.at[p], row_recv.at[slot], {"shard": p})

    @pl.loop(0, n - 1)
    def _(k):
        id_copy(peer_of(k, me, ny, nz), me).start()

    ids_in[me] = wanted[me]
    key_codes(slots, lengths, rowcode, rowbit)
    colcode[...] = rowcode[...].T
    colbit[...] = rowbit[...].T

    @pl.loop(0, n - 1)
    def _(k):
        p = peer_of(k, me, ny, nz)
        id_copy(p, p).wait_recv()

    to_smem = pltpu.make_async_copy(ids_in, ids_sm, sm_sem)
    to_smem.start()
    to_smem.wait()

    def serve(p, out):
        @pl.loop(0, cap // 16)
        def _(t):
            for i in range(16):
                row = t * 16 + i
                out[p, pl.ds(row, 1), :] = table[pl.ds(ids_sm[p, 0, row], 1), :]

    @pl.loop(0, n - 1)
    def _(k):
        p = peer_of(k, me, ny, nz)
        serve(p, sendbuf)
        row_copy(p, me).start()

    serve(me, cache)

    count_words(
        words, feats, bag, lambda key: colcode[:, key:key + 1], lambda key: colbit[:, key:key + 1],
        lax.broadcasted_iota(I32, (samples, cap), 1))

    @pl.loop(0, feats)
    def _(f):
        acc[f] = jnp.zeros(acc.shape[1:], F32)

    count_words(
        wordst, feats, bag, lambda key: rowcode[key:key + 1, :], lambda key: rowbit[key:key + 1, :],
        lax.broadcasted_iota(I32, (cap, samples), 0))
    words_copy = pltpu.make_async_copy(wordst, words_out, words_sem)
    words_copy.start()

    @pl.loop(0, nz)
    def _(j):
        first = plane_from(plane_step(j, nz), z, nz) * ny

        @pl.loop(0, ny)
        def _(i):
            p = first + i

            @pl.when(p != me)
            def _():
                row_copy(p, p).wait_recv()

        rhs = jnp.concatenate(
            [split(cache[first + i] * nibble_scale(first + i)) for i in range(ny)], axis=0)

        @pl.loop(0, feats)
        def _(f):
            word = words[first // 8, f]
            lhs = jnp.concatenate([counts(word, first + i) for i in range(ny)], axis=1)
            acc[f] = acc[f] + dot(lhs, rhs, NN)

    for f in range(feats):
        x0[:, f * emb:(f + 1) * emb] = (acc[f, :, :emb] + acc[f, :, emb:]).astype(BF16)

    @pl.loop(0, n - 1)
    def _(k):
        p = peer_of(k, me, ny, nz)
        id_copy(p, me).wait_send()
        row_copy(p, me).wait_send()

    words_copy.wait()


def fetch(wanted, table, slots, lengths, ny):
    n, cap = wanted.shape
    emb = table.shape[1]
    feats, bag, samples = slots.shape
    keys = feats * bag
    vm = pl.BlockSpec(memory_space=pltpu.VMEM)
    dma = pltpu.SemaphoreType.DMA
    return pl.pallas_call(
        functools.partial(fetch_kernel, n, ny),
        out_shape=[
            jax.ShapeDtypeStruct((samples, feats * emb), BF16),
            jax.ShapeDtypeStruct((n, 1, cap), I32),
            jax.ShapeDtypeStruct((pl.cdiv(n, 8), feats, cap, samples), I32),
        ],
        in_specs=[vm] * 4,
        out_specs=[vm, vm, pl.BlockSpec(memory_space=pl.ANY)],
        scratch_shapes=[
            pltpu.SMEM((n, 1, cap), I32),
            pltpu.VMEM((n, cap, emb), F32),
            pltpu.VMEM((n, cap, emb), F32),
            pltpu.VMEM((pl.cdiv(n, 8), feats, samples, cap), I32),
            pltpu.VMEM((pl.cdiv(n, 8), feats, cap, samples), I32),
            pltpu.VMEM((keys, samples), I32),
            pltpu.VMEM((keys, samples), I32),
            pltpu.VMEM((samples, keys), I32),
            pltpu.VMEM((samples, keys), I32),
            pltpu.VMEM((feats, samples, 2 * emb), F32),
            dma((n,)), dma((n,)), dma((n,)), dma((n,)), dma, dma,
        ],
        compiler_params=pltpu.CompilerParams(
            collective_id=0, has_side_effects=True, vmem_limit_bytes=VMEM_LIMIT),
        name="fetch_pool",
    )(wanted.reshape(n, 1, cap), table, slots, lengths)


def add_refs(out, parts, chunk):
    count = out.shape[0]
    chunk = math.gcd(chunk, count)

    @pl.loop(0, count // chunk)
    def _(t):
        w = pl.ds(t * chunk, chunk)
        total = parts[0][w]
        for p in parts[1:]:
            total = total + p[w]
        out[w] = total


def shares(r, nx, ny):
    per = r // 2
    unit = nx * ny
    second = max(unit, per // 4 // unit * unit)
    return per - second, second


class Stream:
    def __init__(self, local, out, start, size, core, first, second, gz, bufs, sems):
        self.local, self.out, self.start, self.size = local, out, start, size
        self.core, self.first, self.second, self.gz = core, first, second, gz
        self.r1, self.r2, self.b, self.r3, self.c, self.r4 = bufs
        self.sems = sems
        self.share = local.shape[0] // 2
        self.piece = size // first.size
        self.unit = self.piece // second.size
        self.pending = []

    def pair(self, k):
        return self.sems[0].at[k], self.sems[1].at[k]

    def go(self, group, src, dst, k):
        self.pending += spread(group, src, dst, *self.pair(k))

    def come(self, group, src, dst, k):
        arrived(group, src, dst, *self.pair(k))

    def half(self, ref, c):
        return ref.at[pl.ds(c * self.share + self.start, self.size)]

    def core_args(self):
        return self.core, lambda j: self.half(self.local, j), lambda i: self.r1, 0

    def first_args(self):
        return self.first, lambda j: self.r1.at[pl.ds(j * self.piece, self.piece)], lambda i: self.r2.at[i], 1

    def second_args(self):
        return self.second, lambda j: self.b.at[pl.ds(j * self.unit, self.unit)], lambda i: self.r3.at[i], 2

    def z_args(self):
        return self.gz, lambda j: self.c.at[:, j], lambda i: self.r4.at[i], 3

    def at(self, a=None, bb=None):
        at = self.core.me * self.share + self.start
        if a is not None:
            at = at + a * self.piece
        if bb is not None:
            at = at + bb * self.unit
        return at

    def zback_args(self):
        here = lambda i: self.out.at[pl.ds(self.at(self.first.me, self.second.me), self.unit), i]
        return self.gz, lambda j: here(self.gz.me), here, 4

    def second_back_args(self):
        here = lambda i: self.out.at[pl.ds(self.at(self.first.me, i), self.unit)]
        return self.second, lambda j: here(self.second.me), here, 5

    def first_back_args(self):
        here = lambda i: self.out.at[pl.ds(self.at(i), self.piece)]
        return self.first, lambda j: here(self.first.me), here, 6

    def core_back_args(self):
        here = lambda i: self.half(self.out, i)
        return self.core, lambda j: here(self.core.me), here, 7

    def step(self, k):
        args = (self.core_args, self.first_args, self.second_args, self.z_args,
                self.zback_args, self.second_back_args, self.first_back_args, self.core_back_args)
        if k >= 0:
            group, src, dst, i = args[k]()
            self.come(group, src, dst, i)
            if k == 0:
                add_refs(self.r1, [self.r1, self.half(self.local, group.me)], 4)
            elif k < 4:
                out = (None, self.b, self.c, None)[k]
                if k == 3:
                    out = self.out.at[pl.ds(self.at(self.first.me, self.second.me), self.unit), self.gz.me]
                add_refs(out, [src(group.me)] + [dst(j) for _, j in group.others()], 2)
        if k + 1 < len(args):
            self.go(*args[k + 1]())


def dense_kernel(nx, ny, nz, x0, words_in, cot, cw, cb, tw, tb, ow, served,
                 logits, table_out, cross_out, top_out, small_out,
                 g_cross, g_top, small, slot_grads, back, tsum, rt1, rt2,
                 words, y, h, dzb, dyb, dh, dxhl, bufs, sm_bufs, sems):
    n = ny * nz
    cap, emb = back.shape[1:]
    rows = tsum.shape[0]
    feats, samples = dxhl.shape[:2]
    width, top = tw.shape
    dp, me = lax.axis_index("dp"), lax.axis_index("shard")
    x, core, z, yy = dp // 2, dp % 2, me // ny, me % ny
    gx = Group(nx, x, lambda j: {"dp": j * 2 + core})
    gy = Group(ny, yy, lambda j: {"shard": z * ny + j})
    gz = Group(nz, z, lambda j: {"shard": j * ny + yy})
    gc = Group(2, core, lambda j: {"dp": x * 2 + j})
    g_send, g_recv, t_send, t_recv, sm_send, sm_recv, d_send, d_recv, words_sem = sems
    words_copy = pltpu.make_async_copy(words_in, words, words_sem)
    words_copy.start()

    barrier = pltpu.get_barrier_semaphore()

    @pl.loop(0, n - 1)
    def _(k):
        pl.semaphore_signal(barrier, inc=1, device_id={"shard": peer_of(k, me, ny, nz)})

    for grp in (gx, gc):
        for _, j in grp.others():
            pl.semaphore_signal(barrier, inc=1, device_id=grp.address(j))

    streams = []
    for a, (local, out) in enumerate(((g_top, top_out), (g_cross, cross_out))):
        for hh in range(2):
            first, second = ((gx, gy), (gy, gx))[hh]
            s = 2 * a + hh
            part = shares(local.shape[0], nx, ny)
            streams.append(Stream(local, out, hh * part[0], part[hh], gc, first, second, gz, bufs[6 * s:6 * s + 6],
                                  (d_send.at[s], d_recv.at[s])))
    tops, crosses = streams[:2], streams[2:]

    step = min(256, width)
    lanes = step // 128

    def put_small(at, vec):
        for t in range(lanes):
            small[pl.ds(at + t, 1), :] = vec[:, t * 128:(t + 1) * 128]

    def put_dense(out, j, val):
        per = val.shape[1] // 128
        deep = nz // per
        count = step // 8 // deep
        for t in range(per):
            v = val[:, t * 128:(t + 1) * 128].reshape(count, deep, 8, 128)
            for i in range(deep):
                out[pl.ds(j * count, count), i * per + t] = v[:, i]

    @pl.loop(0, width // step)
    def _(j):
        c = pl.ds(pl.multiple_of(j * step, step), step)
        yv = dot(x0[...], cw[:, c], NN) + cb[:, c]
        y[:, c] = yv
        xf = x0[:, c].astype(F32)
        h[:, c] = (xf * yv + xf).astype(BF16)

    cotb = jnp.broadcast_to(cot[...], (128, samples)).T
    lsum = jnp.zeros((samples, 128), F32)
    tstep = min(256, top)
    for j in range(top // tstep):
        c = pl.ds(j * tstep, tstep)
        zv = dot(h[...], tw[:, c], NN) + tb[:, c]
        sig = jax.nn.sigmoid(zv)
        u = zv * sig
        uw = u * ow[:, c]
        cotw = jnp.concatenate([cotb] * (tstep // 128), axis=1)
        for t in range(tstep // 128):
            lsum = lsum + uw[:, t * 128:(t + 1) * 128]
        gow = jnp.sum(u * cotw, axis=0, keepdims=True)
        dz = cotw * ow[:, c] * (sig * (1.0 + zv * (1.0 - sig)))
        gtb = jnp.sum(dz, axis=0, keepdims=True)
        for t in range(tstep // 128):
            at = width // 128 + j * (tstep // 128) + t
            small[pl.ds(at, 1), :] = gtb[:, t * 128:(t + 1) * 128]
            small[pl.ds(at + top // 128, 1), :] = gow[:, t * 128:(t + 1) * 128]
        dzb[:, c] = dz.astype(BF16)
    logits[...] = jnp.sum(lsum.T, axis=0, keepdims=True)

    @pl.loop(0, width // step)
    def _(j):
        c = pl.ds(pl.multiple_of(j * step, step), step)
        put_dense(g_top, j, dot(h[:, c], dzb[...], TN))

    pl.semaphore_wait(barrier, n - 1 + nx - 1 + 1)
    for s in tops:
        s.step(-1)

    @pl.loop(0, width // step)
    def _(j):
        c = pl.ds(pl.multiple_of(j * step, step), step)
        dhv = dot(dzb[...], tw[c, :], NT)
        dh[:, c] = dhv
        dy = dhv * x0[:, c].astype(F32)
        put_small(j * lanes, jnp.sum(dy, axis=0, keepdims=True))
        dyb[:, c] = dy.astype(BF16)

    @pl.loop(0, width // step)
    def _(j):
        c = pl.ds(pl.multiple_of(j * step, step), step)
        put_dense(g_cross, j, dot(x0[:, c], dyb[...], TN))

    for s in crosses:
        s.step(-1)
    pending = []
    s_core, s_x, s_y, s_z, sm1, sm2, sm3 = sm_bufs

    def small_go(k, grp, src, slots_):
        slots_[grp.me] = src[...]
        args = (grp, lambda j: src, lambda i: slots_.at[i], sm_send.at[k], sm_recv.at[k])
        pending.extend(spread(*args))
        return args

    def small_come(args, slots_, out):
        arrived(*args)
        total = slots_[0]
        for i in range(1, slots_.shape[0]):
            total = total + slots_[i]
        out[...] = total

    sm_args = small_go(0, gc, small, s_core)

    @pl.loop(0, width // step)
    def _(j):
        c = pl.ds(pl.multiple_of(j * step, step), step)
        dx = dh[:, c] * (y[:, c] + 1.0) + dot(dyb[...], cw[c, :], NT)
        for t in range(step // emb):
            dxhl[j * (step // emb) + t] = split(dx[:, t * emb:(t + 1) * emb])

    for s in tops:
        s.step(0)
    words_copy.wait()
    for s in crosses:
        s.step(0)
    small_come(sm_args, s_core, sm1)
    sm_args = small_go(1, gx, sm1, s_x)

    def grad_copy(p, slot):
        return remote(slot_grads.at[p], back.at[slot], g_send.at[p], g_recv.at[slot], {"shard": p})

    def plane_to(j):
        return ((z + far_step(j, nz)) % nz) * ny

    def slot_plane(j):
        first = plane_to(j)
        total = jnp.zeros((ny * cap, 2 * emb), F32)
        for f in range(feats):
            word = words[first // 8, f]
            lhs = jnp.concatenate([counts(word, first + i) for i in range(ny)], axis=0)
            total = total + dot(lhs, dxhl[f], NN)
        for i in range(ny):
            part = total[i * cap:(i + 1) * cap]
            slot_grads[first + i] = (part[:, :emb] + part[:, emb:]) * nibble_scale(first + i)

    def send_plane(j):
        @pl.loop(0, ny)
        def _(i):
            p = plane_to(j) + (yy + i + 1) % ny

            @pl.when(p != me)
            def _():
                grad_copy(p, me).start()

        @pl.when(j == nz - 1)
        def _():
            back[me] = slot_grads[me]

    def owner_plane(j):
        first = plane_from(far_step(j, nz), z, nz) * ny

        @pl.loop(0, ny)
        def _(i):
            p = first + i

            @pl.when(p != me)
            def _():
                grad_copy(p, p).wait_recv()

        rhs = jnp.concatenate([split(back[first + i]) for i in range(ny)], axis=0)
        ids = jnp.concatenate([served[first + i] for i in range(ny)], axis=1)
        mstep = min(512, rows)

        @pl.loop(0, rows // mstep)
        def _(t):
            at = t * mstep
            row = lax.broadcasted_iota(I32, (mstep, ny * cap), 0) + at
            hot = jnp.where(row == ids, F32(1), F32(0)).astype(BF16)
            part = dot(hot, rhs, NN)
            part = part[:, :emb] + part[:, emb:]
            w = pl.ds(pl.multiple_of(at, mstep), mstep)
            tsum[w] = jnp.where(j == 0, part, tsum[w] + part)

    def slot_planes(lo, hi, send):
        @pl.loop(lo, min(hi, nz))
        def _(j):
            slot_plane(j)
            if send:
                send_plane(j)

    def send_planes(lo, hi):
        @pl.loop(lo, min(hi, nz))
        def _(j):
            send_plane(j)

    def owner_planes(lo, hi):
        @pl.loop(lo, min(hi, nz))
        def _(j):
            owner_plane(j)

    def steps(which, k):
        for s in which:
            s.step(k)

    early = min(3, nz)
    slot_planes(0, early, True)
    steps(tops, 1)
    slot_planes(early, 6, False)
    steps(tops, 2)
    slot_planes(min(6, nz), nz, False)
    steps(crosses, 1)
    small_come(sm_args, s_x, sm2)
    sm_args = small_go(2, gy, sm2, s_y)
    steps(crosses, 2)
    small_come(sm_args, s_y, sm3)
    sm_args = small_go(3, gz, sm3, s_z)
    steps(tops, 3)
    steps(crosses, 3)
    send_planes(early, nz)
    owner_planes(0, early)
    steps(tops, 4)
    steps(crosses, 4)
    steps(tops, 5)
    steps(crosses, 5)
    small_come(sm_args, s_z, small_out)
    owner_planes(early, 5)
    steps(tops, 6)
    owner_planes(min(5, nz), nz)

    thalf = rows // 2
    tq = thalf // nx
    rows_at = lambda ref, at, size: ref.at[pl.ds(pl.multiple_of(at, size), size)]
    tside = lambda ref, i: rows_at(ref, i * thalf, thalf)
    tpart = lambda ref, i: rows_at(ref, i * tq, tq)
    sem = lambda k: (t_send.at[k], t_recv.at[k])
    tc = (gc, lambda j: tside(tsum, j), lambda i: rt1, *sem(0))
    pending += spread(*tc)
    arrived(*tc)
    rt1[...] = rt1[...] + tside(tsum, core)[...]
    tx = (gx, lambda j: tpart(rt1, j), lambda i: rt2.at[i], *sem(1))
    pending += spread(*tx)
    for s in crosses:
        s.step(6)
    arrived(*tx)
    mine = tpart(tside(table_out, core), x)
    total = tpart(rt1, x)[...]
    for _, j in gx.others():
        total = total + rt2[j]
    mine[...] = total
    there = lambda i: rows_at(table_out, core * thalf + i * tq, tq)
    tb_ = (gx, lambda j: there(x), there, *sem(2))
    pending += spread(*tb_)
    arrived(*tb_)
    tcb = (gc, lambda j: tside(table_out, core), lambda i: tside(table_out, i), *sem(3))
    pending += spread(*tcb)
    for s in streams:
        s.step(7)
    arrived(*tcb)

    for cp in pending + [cp for s in streams for cp in s.pending]:
        cp.wait_send()

    @pl.loop(0, n - 1)
    def _(k):
        grad_copy(peer_of(k, me, ny, nz), me).wait_send()


def dense_and_reduce(x0, words, cot, cw, cb, tw, tb, ow, served, nx, ny, rows):
    samples, width = x0.shape
    top = tw.shape[1]
    feats = words.shape[1]
    n, _, cap = served.shape
    emb = width // feats
    nz = n // ny
    vm = pl.BlockSpec(memory_space=pltpu.VMEM)
    v = pltpu.VMEM
    dma = lambda *s: pltpu.SemaphoreType.DMA(s)
    tiles = lambda *lead: (*lead, 8, 128)
    r_cross = width // 8 * (width // 128) // nz
    r_top = width // 8 * (top // 128) // nz
    sm = ((width + 2 * top) // 128, 128)
    most = max(nx, ny, nz)

    bufs = []
    for r in (r_top, r_cross):
        for (a, b), q in zip(((nx, ny), (ny, nx)), shares(r, nx, ny)):
            p = q // a
            u = p // b
            bufs += [v(tiles(q, nz), F32), v(tiles(a, p, nz), F32), v(tiles(p, nz), F32),
                     v(tiles(b, u, nz), F32), v(tiles(u, nz), F32), v(tiles(nz, u), F32)]
    sm_bufs = [v((k, *sm), F32) for k in (2, nx, ny, nz)] + [v(sm, F32)] * 3
    sems = [dma(n), dma(n), dma(4, most), dma(4, most), dma(4, most), dma(4, most), dma(4, 8, most), dma(4, 8, most),
            pltpu.SemaphoreType.DMA]
    own = [
        v(tiles(r_cross, nz), F32), v(tiles(r_top, nz), F32), v(sm, F32),
        v((n, cap, emb), F32), v((n, cap, emb), F32), v((rows, emb), F32),
        v((rows // 2, emb), F32), v((nx, rows // 2 // nx, emb), F32),
        v(words.shape, I32),
        v((samples, width), F32), v((samples, width), BF16), v((samples, top), BF16), v((samples, width), BF16),
        v((samples, width), F32), v((feats, samples, 2 * emb), BF16),
    ]

    def body(*refs):
        head, rest = refs[:14 + len(own)], refs[14 + len(own):]
        dense_kernel(nx, ny, nz, *head, rest[:24], rest[24:31], rest[31:])

    return pl.pallas_call(
        body,
        out_shape=[
            jax.ShapeDtypeStruct((1, samples), F32),
            jax.ShapeDtypeStruct((rows, emb), F32),
            jax.ShapeDtypeStruct(tiles(r_cross, nz), F32),
            jax.ShapeDtypeStruct(tiles(r_top, nz), F32),
            jax.ShapeDtypeStruct(sm, F32),
        ],
        in_specs=[vm, pl.BlockSpec(memory_space=pl.ANY)] + [vm] * 7,
        out_specs=[vm] * 5,
        scratch_shapes=own + bufs + sm_bufs + sems,
        compiler_params=pltpu.CompilerParams(
            collective_id=1, has_side_effects=True, vmem_limit_bytes=VMEM_LIMIT),
        name="dense_reduce",
    )(x0, words, cot, cw, cb, tw, tb, ow, served)


def publish_kernel(pieces, cross, tops, table, small, logits, cross_out, top_out, table_out,
                   cb_out, tb_out, ow_out, logits_out, cross_buf, top_buf, table_buf, sems):
    logits_out[...] = logits[...]
    reads, writes = [], []
    for src, buf, dst in ((cross, cross_buf, cross_out), (tops, top_buf, top_out), (table, table_buf, table_out)):
        size = src.shape[0] // pieces
        for i in range(pieces):
            w = pl.ds(i * size, size)
            k = len(reads)
            reads.append(pltpu.make_async_copy(src.at[w], buf.at[w], sems.at[0, k]))
            writes.append(pltpu.make_async_copy(buf.at[w], dst.at[w], sems.at[1, k]))
    for read in reads:
        read.start()
    for read, write in zip(reads, writes):
        read.wait()
        write.start()
    at = 0
    for out in (cb_out, tb_out, ow_out):
        out[...] = small[pl.ds(at, out.shape[0]), :]
        at += out.shape[0]
    for write in writes:
        write.wait()


def publish(cross, tops, table, small, logits, width, top):
    hbm = pl.BlockSpec(memory_space=pl.ANY)
    vm = pl.BlockSpec(memory_space=pltpu.VMEM)
    pieces = 4
    return pl.pallas_call(
        functools.partial(publish_kernel, pieces),
        out_shape=[jax.ShapeDtypeStruct(a.shape, F32) for a in (cross, tops, table)]
        + [jax.ShapeDtypeStruct((k // 128, 128), F32) for k in (width, top, top)]
        + [jax.ShapeDtypeStruct(logits.shape, F32)],
        in_specs=[hbm, hbm, hbm, vm, vm],
        out_specs=[hbm, hbm, hbm, vm, vm, vm, vm],
        scratch_shapes=[pltpu.VMEM(a.shape, F32) for a in (cross, tops, table)]
        + [pltpu.SemaphoreType.DMA((2, 3 * pieces))],
        compiler_params=pltpu.CompilerParams(vmem_limit_bytes=VMEM_LIMIT),
        name="publish",
    )(cross, tops, table, small, logits)


def from_tiles(tiles, rows, columns):
    return jnp.transpose(tiles.reshape(rows // 8, columns // 128, 8, 128), (0, 2, 1, 3)).reshape(rows, columns)


def on_device(table, cross_weight, cross_bias, top_weight, top_bias, out_weight, wanted, slots, lengths, logit_grad,
              nx=NX, ny=NY):
    width, top = top_weight.shape
    keys, live = jnp.transpose(slots, (1, 2, 0)), lengths.T
    x0, served, words = fetch(wanted[0], table, keys, live, ny)
    logits, table_grad, cross, tops, vecs = dense_and_reduce(
        x0, words, logit_grad[None], cross_weight, cross_bias[None], top_weight, top_bias[None], out_weight[None],
        served, nx, ny, table.shape[0])
    cross, tops, table_grad, g_cb, g_tb, g_ow, logits = publish(
        cross, tops, table_grad, vecs, logits, width, top)
    return (logits[0], from_tiles(cross, width, width), from_tiles(tops, width, top),
            g_cb.reshape(-1), g_tb.reshape(-1), g_ow.reshape(-1), table_grad)


def solution(mesh):
    placed = (
        P("shard", None),
        P(),
        P(),
        P(),
        P(),
        P(),
        P(("dp", "shard"), None, None),
        P(("dp", "shard"), None, None),
        P(("dp", "shard"), None),
        P(("dp", "shard")),
    )
    return jax.shard_map(
        on_device,
        mesh=mesh,
        in_specs=placed,
        out_specs=(P(("dp", "shard")), P(), P(), P(), P(), P(), P("shard", None)),
        check_vma=False,
    )
```

```python
import functools
import math

import jax
import jax.numpy as jnp
from jax import lax
from jax.experimental import pallas as pl
from jax.experimental.pallas import tpu as pltpu
from jax.sharding import PartitionSpec as P

F32, BF16, I32 = jnp.float32, jnp.bfloat16, jnp.int32
VMEM_LIMIT = 60 * 1024 * 1024
NX, NY = 4, 4
NN = ((1,), (0,))
NT = ((1,), (1,))
TN = ((0,), (0,))


def dot(a, b, dims):
    return lax.dot_general(a, b, (dims, ((), ())), preferred_element_type=F32)


def split(x):
    hi = x.astype(BF16)
    lo = (x - hi.astype(F32)).astype(BF16)
    return jnp.concatenate([hi, lo], axis=1)


def nibble_mask(o):
    return jnp.left_shift(jnp.int32(15), (o % 8) * 4)


def nibble_scale(o):
    k = o % 8
    s = jnp.where((k & 1) == 1, F32(2.0**-4), F32(1.0))
    s = s * jnp.where((k & 2) == 2, F32(2.0**-8), F32(1.0))
    return s * jnp.where((k & 4) == 4, F32(2.0**-16), F32(1.0))


def key_codes(slots, lengths, rowcode, rowbit):
    feats, bag, samples = slots.shape
    for b in range(bag):
        slot = slots[:, b, :]
        owner = slot >> 7
        rowcode[pl.ds(b * feats, feats), :] = jnp.where(
            lengths[...] > b, (slot & 127) + ((owner >> 3) << 7), -1)
        rowbit[pl.ds(b * feats, feats), :] = jnp.left_shift(jnp.ones_like(owner), (owner & 7) << 2)


def count_words(words, feats, bag, code_of, bit_of, place):
    groups, cap = words.shape[0], 128
    for f in range(feats):
        sums = [jnp.zeros(place.shape, I32)] * groups
        for b in range(bag):
            key = b * feats + f
            code = jnp.broadcast_to(code_of(key), place.shape) - place
            bit = jnp.broadcast_to(bit_of(key), place.shape)
            for w in range(groups):
                sums[w] = sums[w] + jnp.where(code == w * cap, bit, 0)
        for w in range(groups):
            words[w, f] = sums[w]


def counts(word, o):
    return (word & nibble_mask(o)).astype(F32).astype(BF16)


class Group:
    def __init__(self, size, me, address):
        self.size, self.me, self.address = size, me, address

    def others(self):
        return [(d, (self.me + d) % self.size) for d in range(1, self.size)]


def plane_step(j, nz):
    return ((j + 1) // 2 * (2 * (j % 2) - 1) + nz) % nz


def far_step(j, nz):
    if nz == 8:
        q = (j + 1) // 2
        return (4 + (q * q * q + 3 * q * q + 3 * q) % 5 * (1 - 2 * (j % 2))) % 8
    return nz // 2 + (j // 2 + j % 2) * (1 - 2 * (j % 2))


def peer_of(k, me, ny, nz):
    z = (me // ny + plane_step((k + 1) // ny, nz)) % nz
    y = (me % ny + (k + 1) % ny) % ny
    return z * ny + y


def plane_from(step, z, nz):
    return (z - step + 2 * nz) % nz


def remote(src, dst, send, recv, to):
    return pltpu.make_async_remote_copy(
        src_ref=src, dst_ref=dst, send_sem=send, recv_sem=recv, device_id=to)


def spread(group, src, dst, send, recv):
    copies = []
    for d, j in group.others():
        cp = remote(src(j), dst(group.me), send.at[d], recv.at[group.me], group.address(j))
        cp.start()
        copies.append(cp)
    return copies


def arrived(group, src, dst, send, recv):
    for d, j in group.others():
        remote(src(j), dst(j), send.at[d], recv.at[j], group.address(j)).wait_recv()


def fetch_kernel(n, ny, wanted, table, slots, lengths, x0, ids_in, words_out,
                 ids_sm, sendbuf, cache, words, wordst, rowcode, rowbit, colcode, colbit, acc,
                 id_send, id_recv, row_send, row_recv, sm_sem, words_sem):
    nz = n // ny
    cap, emb = cache.shape[1:]
    feats, bag, samples = slots.shape
    me = lax.axis_index("shard")
    z = me // ny
    barrier = pltpu.get_barrier_semaphore()

    @pl.loop(0, n - 1)
    def _(k):
        pl.semaphore_signal(barrier, inc=1, device_id={"shard": peer_of(k, me, ny, nz)})

    pl.semaphore_wait(barrier, n - 1)

    def id_copy(p, slot):
        return remote(wanted.at[p], ids_in.at[slot], id_send.at[p], id_recv.at[slot], {"shard": p})

    def row_copy(p, slot):
        return remote(sendbuf.at[p], cache.at[slot], row_send.at[p], row_recv.at[slot], {"shard": p})

    @pl.loop(0, n - 1)
    def _(k):
        id_copy(peer_of(k, me, ny, nz), me).start()

    ids_in[me] = wanted[me]
    key_codes(slots, lengths, rowcode, rowbit)
    colcode[...] = rowcode[...].T
    colbit[...] = rowbit[...].T

    @pl.loop(0, n - 1)
    def _(k):
        p = peer_of(k, me, ny, nz)
        id_copy(p, p).wait_recv()

    to_smem = pltpu.make_async_copy(ids_in, ids_sm, sm_sem)
    to_smem.start()
    to_smem.wait()

    def serve(p, out):
        @pl.loop(0, cap // 16)
        def _(t):
            for i in range(16):
                row = t * 16 + i
                out[p, pl.ds(row, 1), :] = table[pl.ds(ids_sm[p, 0, row], 1), :]

    @pl.loop(0, n - 1)
    def _(k):
        p = peer_of(k, me, ny, nz)
        serve(p, sendbuf)
        row_copy(p, me).start()

    serve(me, cache)

    count_words(
        words, feats, bag, lambda key: colcode[:, key:key + 1], lambda key: colbit[:, key:key + 1],
        lax.broadcasted_iota(I32, (samples, cap), 1))

    @pl.loop(0, feats)
    def _(f):
        acc[f] = jnp.zeros(acc.shape[1:], F32)

    count_words(
        wordst, feats, bag, lambda key: rowcode[key:key + 1, :], lambda key: rowbit[key:key + 1, :],
        lax.broadcasted_iota(I32, (cap, samples), 0))
    words_copy = pltpu.make_async_copy(wordst, words_out, words_sem)
    words_copy.start()

    @pl.loop(0, nz)
    def _(j):
        first = plane_from(plane_step(j, nz), z, nz) * ny

        @pl.loop(0, ny)
        def _(i):
            p = first + i

            @pl.when(p != me)
            def _():
                row_copy(p, p).wait_recv()

        rhs = jnp.concatenate(
            [split(cache[first + i] * nibble_scale(first + i)) for i in range(ny)], axis=0)

        @pl.loop(0, feats)
        def _(f):
            word = words[first // 8, f]
            lhs = jnp.concatenate([counts(word, first + i) for i in range(ny)], axis=1)
            acc[f] = acc[f] + dot(lhs, rhs, NN)

    for f in range(feats):
        x0[:, f * emb:(f + 1) * emb] = (acc[f, :, :emb] + acc[f, :, emb:]).astype(BF16)

    @pl.loop(0, n - 1)
    def _(k):
        p = peer_of(k, me, ny, nz)
        id_copy(p, me).wait_send()
        row_copy(p, me).wait_send()

    words_copy.wait()


def fetch(wanted, table, slots, lengths, ny):
    n, cap = wanted.shape
    emb = table.shape[1]
    feats, bag, samples = slots.shape
    keys = feats * bag
    vm = pl.BlockSpec(memory_space=pltpu.VMEM)
    dma = pltpu.SemaphoreType.DMA
    return pl.pallas_call(
        functools.partial(fetch_kernel, n, ny),
        out_shape=[
            jax.ShapeDtypeStruct((samples, feats * emb), BF16),
            jax.ShapeDtypeStruct((n, 1, cap), I32),
            jax.ShapeDtypeStruct((pl.cdiv(n, 8), feats, cap, samples), I32),
        ],
        in_specs=[vm] * 4,
        out_specs=[vm, vm, pl.BlockSpec(memory_space=pl.ANY)],
        scratch_shapes=[
            pltpu.SMEM((n, 1, cap), I32),
            pltpu.VMEM((n, cap, emb), F32),
            pltpu.VMEM((n, cap, emb), F32),
            pltpu.VMEM((pl.cdiv(n, 8), feats, samples, cap), I32),
            pltpu.VMEM((pl.cdiv(n, 8), feats, cap, samples), I32),
            pltpu.VMEM((keys, samples), I32),
            pltpu.VMEM((keys, samples), I32),
            pltpu.VMEM((samples, keys), I32),
            pltpu.VMEM((samples, keys), I32),
            pltpu.VMEM((feats, samples, 2 * emb), F32),
            dma((n,)), dma((n,)), dma((n,)), dma((n,)), dma, dma,
        ],
        compiler_params=pltpu.CompilerParams(
            collective_id=0, has_side_effects=True, vmem_limit_bytes=VMEM_LIMIT),
        name="fetch_pool",
    )(wanted.reshape(n, 1, cap), table, slots, lengths)


def add_refs(out, parts, chunk):
    count = out.shape[0]
    chunk = math.gcd(chunk, count)

    @pl.loop(0, count // chunk)
    def _(t):
        w = pl.ds(t * chunk, chunk)
        total = parts[0][w]
        for p in parts[1:]:
            total = total + p[w]
        out[w] = total


def shares(r, nx, ny):
    per = r // 2
    unit = nx * ny
    second = max(unit, per // 2 // unit * unit)
    return per - second, second


class Stream:
    def __init__(self, local, out, start, size, core, first, second, gz, bufs, sems):
        self.local, self.out, self.start, self.size = local, out, start, size
        self.core, self.first, self.second, self.gz = core, first, second, gz
        self.r1, self.r2, self.b, self.r3, self.c, self.r4 = bufs
        self.sems = sems
        self.share = local.shape[0] // 2
        self.piece = size // first.size
        self.unit = self.piece // second.size
        self.pending = []

    def pair(self, k):
        return self.sems[0].at[k], self.sems[1].at[k]

    def go(self, group, src, dst, k):
        self.pending += spread(group, src, dst, *self.pair(k))

    def come(self, group, src, dst, k):
        arrived(group, src, dst, *self.pair(k))

    def half(self, ref, c):
        return ref.at[pl.ds(c * self.share + self.start, self.size)]

    def core_args(self):
        return self.core, lambda j: self.half(self.local, j), lambda i: self.r1, 0

    def first_args(self):
        return self.first, lambda j: self.r1.at[pl.ds(j * self.piece, self.piece)], lambda i: self.r2.at[i], 1

    def second_args(self):
        return self.second, lambda j: self.b.at[pl.ds(j * self.unit, self.unit)], lambda i: self.r3.at[i], 2

    def z_args(self):
        return self.gz, lambda j: self.c.at[:, j], lambda i: self.r4.at[i], 3

    def at(self, a=None, bb=None):
        at = self.core.me * self.share + self.start
        if a is not None:
            at = at + a * self.piece
        if bb is not None:
            at = at + bb * self.unit
        return at

    def zback_args(self):
        here = lambda i: self.out.at[pl.ds(self.at(self.first.me, self.second.me), self.unit), i]
        return self.gz, lambda j: here(self.gz.me), here, 4

    def second_back_args(self):
        here = lambda i: self.out.at[pl.ds(self.at(self.first.me, i), self.unit)]
        return self.second, lambda j: here(self.second.me), here, 5

    def first_back_args(self):
        here = lambda i: self.out.at[pl.ds(self.at(i), self.piece)]
        return self.first, lambda j: here(self.first.me), here, 6

    def core_back_args(self):
        here = lambda i: self.half(self.out, i)
        return self.core, lambda j: here(self.core.me), here, 7

    def step(self, k):
        args = (self.core_args, self.first_args, self.second_args, self.z_args,
                self.zback_args, self.second_back_args, self.first_back_args, self.core_back_args)
        if k >= 0:
            group, src, dst, i = args[k]()
            self.come(group, src, dst, i)
            if k == 0:
                add_refs(self.r1, [self.r1, self.half(self.local, group.me)], 4)
            elif k < 4:
                out = (None, self.b, self.c, None)[k]
                if k == 3:
                    out = self.out.at[pl.ds(self.at(self.first.me, self.second.me), self.unit), self.gz.me]
                add_refs(out, [src(group.me)] + [dst(j) for _, j in group.others()], 2)
        if k + 1 < len(args):
            self.go(*args[k + 1]())


def dense_kernel(nx, ny, nz, x0, words_in, cot, cw, cb, tw, tb, ow, served,
                 logits, table_out, cross_hbm, top_hbm, small_out,
                 cross_out, top_out,
                 g_cross, g_top, small, slot_grads, back, tsum, rt1, rt2,
                 words, y, h, dzb, dyb, dh, dxhl, bufs, sm_bufs, sems):
    n = ny * nz
    cap, emb = back.shape[1:]
    rows = tsum.shape[0]
    feats, samples = dxhl.shape[:2]
    width, top = tw.shape
    dp, me = lax.axis_index("dp"), lax.axis_index("shard")
    x, core, z, yy = dp // 2, dp % 2, me // ny, me % ny
    gx = Group(nx, x, lambda j: {"dp": j * 2 + core})
    gy = Group(ny, yy, lambda j: {"shard": z * ny + j})
    gz = Group(nz, z, lambda j: {"shard": j * ny + yy})
    gc = Group(2, core, lambda j: {"dp": x * 2 + j})
    g_send, g_recv, t_send, t_recv, sm_send, sm_recv, d_send, d_recv, words_sem, out_sems = sems
    words_copy = pltpu.make_async_copy(words_in, words, words_sem)
    words_copy.start()

    barrier = pltpu.get_barrier_semaphore()

    @pl.loop(0, n - 1)
    def _(k):
        pl.semaphore_signal(barrier, inc=1, device_id={"shard": peer_of(k, me, ny, nz)})

    for grp in (gx, gc):
        for _, j in grp.others():
            pl.semaphore_signal(barrier, inc=1, device_id=grp.address(j))

    streams = []
    for a, (local, out) in enumerate(((g_top, top_out), (g_cross, cross_out))):
        for hh in range(2):
            first, second = ((gx, gy), (gy, gx))[hh]
            s = 2 * a + hh
            part = shares(local.shape[0], nx, ny)
            streams.append(Stream(local, out, hh * part[0], part[hh], gc, first, second, gz, bufs[6 * s:6 * s + 6],
                                  (d_send.at[s], d_recv.at[s])))
    tops, crosses = streams[:2], streams[2:]

    step = min(256, width)
    lanes = step // 128

    def put_small(at, vec):
        for t in range(lanes):
            small[pl.ds(at + t, 1), :] = vec[:, t * 128:(t + 1) * 128]

    def put_dense(out, j, val):
        per = val.shape[1] // 128
        deep = nz // per
        count = step // 8 // deep
        for t in range(per):
            v = val[:, t * 128:(t + 1) * 128].reshape(count, deep, 8, 128)
            for i in range(deep):
                out[pl.ds(j * count, count), i * per + t] = v[:, i]

    @pl.loop(0, width // step)
    def _(j):
        c = pl.ds(pl.multiple_of(j * step, step), step)
        yv = dot(x0[...], cw[:, c], NN) + cb[:, c]
        y[:, c] = yv
        xf = x0[:, c].astype(F32)
        h[:, c] = (xf * yv + xf).astype(BF16)

    cotb = jnp.broadcast_to(cot[...], (128, samples)).T
    lsum = jnp.zeros((samples, 128), F32)
    tstep = min(256, top)
    for j in range(top // tstep):
        c = pl.ds(j * tstep, tstep)
        zv = dot(h[...], tw[:, c], NN) + tb[:, c]
        sig = jax.nn.sigmoid(zv)
        u = zv * sig
        uw = u * ow[:, c]
        cotw = jnp.concatenate([cotb] * (tstep // 128), axis=1)
        for t in range(tstep // 128):
            lsum = lsum + uw[:, t * 128:(t + 1) * 128]
        gow = jnp.sum(u * cotw, axis=0, keepdims=True)
        dz = cotw * ow[:, c] * (sig * (1.0 + zv * (1.0 - sig)))
        gtb = jnp.sum(dz, axis=0, keepdims=True)
        for t in range(tstep // 128):
            at = width // 128 + j * (tstep // 128) + t
            small[pl.ds(at, 1), :] = gtb[:, t * 128:(t + 1) * 128]
            small[pl.ds(at + top // 128, 1), :] = gow[:, t * 128:(t + 1) * 128]
        dzb[:, c] = dz.astype(BF16)
    logits[...] = jnp.sum(lsum.T, axis=0, keepdims=True)

    @pl.loop(0, width // step)
    def _(j):
        c = pl.ds(pl.multiple_of(j * step, step), step)
        put_dense(g_top, j, dot(h[:, c], dzb[...], TN))

    pl.semaphore_wait(barrier, n - 1 + nx - 1 + 1)
    for s in tops:
        s.step(-1)

    @pl.loop(0, width // step)
    def _(j):
        c = pl.ds(pl.multiple_of(j * step, step), step)
        dhv = dot(dzb[...], tw[c, :], NT)
        dh[:, c] = dhv
        dy = dhv * x0[:, c].astype(F32)
        put_small(j * lanes, jnp.sum(dy, axis=0, keepdims=True))
        dyb[:, c] = dy.astype(BF16)

    @pl.loop(0, width // step)
    def _(j):
        c = pl.ds(pl.multiple_of(j * step, step), step)
        put_dense(g_cross, j, dot(x0[:, c], dyb[...], TN))

    for s in crosses:
        s.step(-1)
    pending = []
    s_core, s_x, s_y, s_z, sm1, sm2, sm3 = sm_bufs

    def small_go(k, grp, src, slots_):
        slots_[grp.me] = src[...]
        args = (grp, lambda j: src, lambda i: slots_.at[i], sm_send.at[k], sm_recv.at[k])
        pending.extend(spread(*args))
        return args

    def small_come(args, slots_, out):
        arrived(*args)
        total = slots_[0]
        for i in range(1, slots_.shape[0]):
            total = total + slots_[i]
        out[...] = total

    sm_args = small_go(0, gc, small, s_core)

    @pl.loop(0, width // step)
    def _(j):
        c = pl.ds(pl.multiple_of(j * step, step), step)
        dx = dh[:, c] * (y[:, c] + 1.0) + dot(dyb[...], cw[c, :], NT)
        for t in range(step // emb):
            dxhl[j * (step // emb) + t] = split(dx[:, t * emb:(t + 1) * emb])

    for s in tops:
        s.step(0)
    words_copy.wait()
    for s in crosses:
        s.step(0)
    small_come(sm_args, s_core, sm1)
    sm_args = small_go(1, gx, sm1, s_x)

    def grad_copy(p, slot):
        return remote(slot_grads.at[p], back.at[slot], g_send.at[p], g_recv.at[slot], {"shard": p})

    def plane_to(j):
        return ((z + far_step(j, nz)) % nz) * ny

    def slot_plane(j):
        first = plane_to(j)
        total = jnp.zeros((ny * cap, 2 * emb), F32)
        for f in range(feats):
            word = words[first // 8, f]
            lhs = jnp.concatenate([counts(word, first + i) for i in range(ny)], axis=0)
            total = total + dot(lhs, dxhl[f], NN)
        for i in range(ny):
            part = total[i * cap:(i + 1) * cap]
            slot_grads[first + i] = (part[:, :emb] + part[:, emb:]) * nibble_scale(first + i)

    def send_plane(j):
        @pl.loop(0, ny)
        def _(i):
            p = plane_to(j) + (yy + i + 1) % ny

            @pl.when(p != me)
            def _():
                grad_copy(p, me).start()

        @pl.when(j == nz - 1)
        def _():
            back[me] = slot_grads[me]

    def owner_plane(j):
        first = plane_from(far_step(j, nz), z, nz) * ny

        @pl.loop(0, ny)
        def _(i):
            p = first + i

            @pl.when(p != me)
            def _():
                grad_copy(p, p).wait_recv()

        rhs = jnp.concatenate([split(back[first + i]) for i in range(ny)], axis=0)
        ids = jnp.concatenate([served[first + i] for i in range(ny)], axis=1)
        mstep = min(512, rows)

        @pl.loop(0, rows // mstep)
        def _(t):
            at = t * mstep
            row = lax.broadcasted_iota(I32, (mstep, ny * cap), 0) + at
            hot = jnp.where(row == ids, F32(1), F32(0)).astype(BF16)
            part = dot(hot, rhs, NN)
            part = part[:, :emb] + part[:, emb:]
            w = pl.ds(pl.multiple_of(at, mstep), mstep)
            tsum[w] = jnp.where(j == 0, part, tsum[w] + part)

    def slot_planes(lo, hi, send):
        @pl.loop(lo, min(hi, nz))
        def _(j):
            slot_plane(j)
            if send:
                send_plane(j)

    def send_planes(lo, hi):
        @pl.loop(lo, min(hi, nz))
        def _(j):
            send_plane(j)

    def owner_planes(lo, hi):
        @pl.loop(lo, min(hi, nz))
        def _(j):
            owner_plane(j)

    def steps(which, k):
        for s in which:
            s.step(k)

    early = min(3, nz)
    slot_planes(0, early, True)
    steps(tops, 1)
    slot_planes(early, 5, False)
    steps(crosses, 1)
    small_come(sm_args, s_x, sm2)
    sm_args = small_go(2, gy, sm2, s_y)
    steps(tops, 2)
    slot_planes(min(5, nz), 7, False)
    steps(crosses, 2)
    small_come(sm_args, s_y, sm3)
    sm_args = small_go(3, gz, sm3, s_z)
    slot_planes(min(7, nz), nz, False)
    steps(tops, 3)
    steps(crosses, 3)
    send_planes(early, nz)
    steps(tops, 4)
    steps(crosses, 4)
    owner_planes(0, early)
    steps(tops, 5)
    steps(crosses, 5)
    small_come(sm_args, s_z, small_out)
    owner_planes(early, 5)
    steps(tops, 6)
    owner_planes(min(5, nz), nz)

    thalf = rows // 2
    tq = thalf // nx
    rows_at = lambda ref, at, size: ref.at[pl.ds(pl.multiple_of(at, size), size)]
    tside = lambda ref, i: rows_at(ref, i * thalf, thalf)
    tpart = lambda ref, i: rows_at(ref, i * tq, tq)
    sem = lambda k: (t_send.at[k], t_recv.at[k])
    tc = (gc, lambda j: tside(tsum, j), lambda i: rt1, *sem(0))
    pending += spread(*tc)
    arrived(*tc)
    rt1[...] = rt1[...] + tside(tsum, core)[...]
    tx = (gx, lambda j: tpart(rt1, j), lambda i: rt2.at[i], *sem(1))
    pending += spread(*tx)
    for s in crosses:
        s.step(6)
    arrived(*tx)
    mine = tpart(tside(table_out, core), x)
    total = tpart(rt1, x)[...]
    for _, j in gx.others():
        total = total + rt2[j]
    mine[...] = total
    there = lambda i: rows_at(table_out, core * thalf + i * tq, tq)
    tb_ = (gx, lambda j: there(x), there, *sem(2))
    pending += spread(*tb_)
    flushes = []
    for i, (which, src, dst) in enumerate(((tops, top_out, top_hbm), (crosses, cross_out, cross_hbm))):
        steps(which, 7)
        flushes.append(pltpu.make_async_copy(src, dst, out_sems.at[i]))
        flushes[-1].start()
    arrived(*tb_)
    tcb = (gc, lambda j: tside(table_out, core), lambda i: tside(table_out, i), *sem(3))
    pending += spread(*tcb)
    arrived(*tcb)
    for cp in flushes:
        cp.wait()

    for cp in pending + [cp for s in streams for cp in s.pending]:
        cp.wait_send()

    @pl.loop(0, n - 1)
    def _(k):
        grad_copy(peer_of(k, me, ny, nz), me).wait_send()


def dense_and_reduce(x0, words, cot, cw, cb, tw, tb, ow, served, nx, ny, rows):
    samples, width = x0.shape
    top = tw.shape[1]
    feats = words.shape[1]
    n, _, cap = served.shape
    emb = width // feats
    nz = n // ny
    vm = pl.BlockSpec(memory_space=pltpu.VMEM)
    v = pltpu.VMEM
    dma = lambda *s: pltpu.SemaphoreType.DMA(s)
    tiles = lambda *lead: (*lead, 8, 128)
    r_cross = width // 8 * (width // 128) // nz
    r_top = width // 8 * (top // 128) // nz
    sm = ((width + 2 * top) // 128, 128)
    most = max(nx, ny, nz)

    bufs = []
    for r in (r_top, r_cross):
        for (a, b), q in zip(((nx, ny), (ny, nx)), shares(r, nx, ny)):
            p = q // a
            u = p // b
            bufs += [v(tiles(q, nz), F32), v(tiles(a, p, nz), F32), v(tiles(p, nz), F32),
                     v(tiles(b, u, nz), F32), v(tiles(u, nz), F32), v(tiles(nz, u), F32)]
    sm_bufs = [v((k, *sm), F32) for k in (2, nx, ny, nz)] + [v(sm, F32)] * 3
    sems = [dma(n), dma(n), dma(4, most), dma(4, most), dma(4, most), dma(4, most), dma(4, 8, most), dma(4, 8, most),
            pltpu.SemaphoreType.DMA, dma(2)]
    own = [
        v(tiles(r_cross, nz), F32), v(tiles(r_top, nz), F32),
        v(tiles(r_cross, nz), F32), v(tiles(r_top, nz), F32), v(sm, F32),
        v((n, cap, emb), F32), v((n, cap, emb), F32), v((rows, emb), F32),
        v((rows // 2, emb), F32), v((nx, rows // 2 // nx, emb), F32),
        v(words.shape, I32),
        v((samples, width), F32), v((samples, width), BF16), v((samples, top), BF16), v((samples, width), BF16),
        v((samples, width), F32), v((feats, samples, 2 * emb), BF16),
    ]

    def body(*refs):
        head, rest = refs[:14 + len(own)], refs[14 + len(own):]
        dense_kernel(nx, ny, nz, *head, rest[:24], rest[24:31], rest[31:])

    return pl.pallas_call(
        body,
        out_shape=[
            jax.ShapeDtypeStruct((1, samples), F32),
            jax.ShapeDtypeStruct((rows, emb), F32),
            jax.ShapeDtypeStruct(tiles(r_cross, nz), F32),
            jax.ShapeDtypeStruct(tiles(r_top, nz), F32),
            jax.ShapeDtypeStruct(sm, F32),
        ],
        in_specs=[vm, pl.BlockSpec(memory_space=pl.ANY)] + [vm] * 7,
        out_specs=[vm, vm, pl.BlockSpec(memory_space=pl.ANY), pl.BlockSpec(memory_space=pl.ANY), vm],
        scratch_shapes=own + bufs + sm_bufs + sems,
        compiler_params=pltpu.CompilerParams(
            collective_id=1, has_side_effects=True, vmem_limit_bytes=VMEM_LIMIT),
        name="dense_reduce",
    )(x0, words, cot, cw, cb, tw, tb, ow, served)


def publish_kernel(pieces, cross, tops, table, small, logits, cross_out, top_out, table_out,
                   cb_out, tb_out, ow_out, logits_out, cross_buf, top_buf, table_buf, sems):
    logits_out[...] = logits[...]
    reads, writes = [], []
    for src, buf, dst in ((cross, cross_buf, cross_out), (tops, top_buf, top_out), (table, table_buf, table_out)):
        size = src.shape[0] // pieces
        for i in range(pieces):
            w = pl.ds(i * size, size)
            k = len(reads)
            reads.append(pltpu.make_async_copy(src.at[w], buf.at[w], sems.at[0, k]))
            writes.append(pltpu.make_async_copy(buf.at[w], dst.at[w], sems.at[1, k]))
    for read in reads:
        read.start()
    for read, write in zip(reads, writes):
        read.wait()
        write.start()
    at = 0
    for out in (cb_out, tb_out, ow_out):
        out[...] = small[pl.ds(at, out.shape[0]), :]
        at += out.shape[0]
    for write in writes:
        write.wait()


def publish(cross, tops, table, small, logits, width, top):
    hbm = pl.BlockSpec(memory_space=pl.ANY)
    vm = pl.BlockSpec(memory_space=pltpu.VMEM)
    pieces = 4
    return pl.pallas_call(
        functools.partial(publish_kernel, pieces),
        out_shape=[jax.ShapeDtypeStruct(a.shape, F32) for a in (cross, tops, table)]
        + [jax.ShapeDtypeStruct((k // 128, 128), F32) for k in (width, top, top)]
        + [jax.ShapeDtypeStruct(logits.shape, F32)],
        in_specs=[hbm, hbm, hbm, vm, vm],
        out_specs=[hbm, hbm, hbm, vm, vm, vm, vm],
        scratch_shapes=[pltpu.VMEM(a.shape, F32) for a in (cross, tops, table)]
        + [pltpu.SemaphoreType.DMA((2, 3 * pieces))],
        compiler_params=pltpu.CompilerParams(vmem_limit_bytes=VMEM_LIMIT),
        name="publish",
    )(cross, tops, table, small, logits)


def from_tiles(tiles, rows, columns):
    return jnp.transpose(tiles.reshape(rows // 8, columns // 128, 8, 128), (0, 2, 1, 3)).reshape(rows, columns)


def on_device(table, cross_weight, cross_bias, top_weight, top_bias, out_weight, wanted, slots, lengths, logit_grad,
              nx=NX, ny=NY):
    width, top = top_weight.shape
    keys, live = jnp.transpose(slots, (1, 2, 0)), lengths.T
    x0, served, words = fetch(wanted[0], table, keys, live, ny)
    logits, table_grad, cross, tops, vecs = dense_and_reduce(
        x0, words, logit_grad[None], cross_weight, cross_bias[None], top_weight, top_bias[None], out_weight[None],
        served, nx, ny, table.shape[0])
    cross, tops, table_grad, g_cb, g_tb, g_ow, logits = publish(
        cross, tops, table_grad, vecs, logits, width, top)
    return (logits[0], from_tiles(cross, width, width), from_tiles(tops, width, top),
            g_cb.reshape(-1), g_tb.reshape(-1), g_ow.reshape(-1), table_grad)


def solution(mesh):
    placed = (
        P("shard", None),
        P(),
        P(),
        P(),
        P(),
        P(),
        P(("dp", "shard"), None, None),
        P(("dp", "shard"), None, None),
        P(("dp", "shard"), None),
        P(("dp", "shard")),
    )
    return jax.shard_map(
        on_device,
        mesh=mesh,
        in_specs=placed,
        out_specs=(P(("dp", "shard")), P(), P(), P(), P(), P(), P("shard", None)),
        check_vma=False,
    )
```

```python
import functools
import math

import jax
import jax.numpy as jnp
from jax import lax
from jax.experimental import pallas as pl
from jax.experimental.pallas import tpu as pltpu
from jax.sharding import PartitionSpec as P

F32, BF16, I32 = jnp.float32, jnp.bfloat16, jnp.int32
VMEM_LIMIT = 60 * 1024 * 1024
NX, NY = 4, 4
NN = ((1,), (0,))
NT = ((1,), (1,))
TN = ((0,), (0,))


def dot(a, b, dims):
    return lax.dot_general(a, b, (dims, ((), ())), preferred_element_type=F32)


def split(x):
    hi = x.astype(BF16)
    lo = (x - hi.astype(F32)).astype(BF16)
    return jnp.concatenate([hi, lo], axis=1)


def nibble_mask(o):
    return jnp.left_shift(jnp.int32(15), (o % 8) * 4)


def nibble_scale(o):
    k = o % 8
    s = jnp.where((k & 1) == 1, F32(2.0**-4), F32(1.0))
    s = s * jnp.where((k & 2) == 2, F32(2.0**-8), F32(1.0))
    return s * jnp.where((k & 4) == 4, F32(2.0**-16), F32(1.0))


def key_codes(slots, lengths, rowcode, rowbit):
    feats, bag, samples = slots.shape
    for b in range(bag):
        slot = slots[:, b, :]
        owner = slot >> 7
        rowcode[pl.ds(b * feats, feats), :] = jnp.where(
            lengths[...] > b, (slot & 127) + ((owner >> 3) << 7), -1)
        rowbit[pl.ds(b * feats, feats), :] = jnp.left_shift(jnp.ones_like(owner), (owner & 7) << 2)


def count_words(words, feats, bag, code_of, bit_of, place):
    groups, cap = words.shape[0], 128
    for f in range(feats):
        sums = [jnp.zeros(place.shape, I32)] * groups
        for b in range(bag):
            key = b * feats + f
            code = jnp.broadcast_to(code_of(key), place.shape) - place
            bit = jnp.broadcast_to(bit_of(key), place.shape)
            for w in range(groups):
                sums[w] = sums[w] + jnp.where(code == w * cap, bit, 0)
        for w in range(groups):
            words[w, f] = sums[w]


def counts(word, o):
    return (word & nibble_mask(o)).astype(F32).astype(BF16)


class Group:
    def __init__(self, size, me, address):
        self.size, self.me, self.address = size, me, address

    def others(self):
        return [(d, (self.me + d) % self.size) for d in range(1, self.size)]


def plane_step(j, nz):
    return ((j + 1) // 2 * (2 * (j % 2) - 1) + nz) % nz


def far_step(j, nz):
    if nz == 8:
        q = (j + 1) // 2
        return (4 + (q * q * q + 3 * q * q + 3 * q) % 5 * (1 - 2 * (j % 2))) % 8
    return nz // 2 + (j // 2 + j % 2) * (1 - 2 * (j % 2))


def peer_of(k, me, ny, nz):
    z = (me // ny + plane_step((k + 1) // ny, nz)) % nz
    y = (me % ny + (k + 1) % ny) % ny
    return z * ny + y


def plane_from(step, z, nz):
    return (z - step + 2 * nz) % nz


def remote(src, dst, send, recv, to):
    return pltpu.make_async_remote_copy(
        src_ref=src, dst_ref=dst, send_sem=send, recv_sem=recv, device_id=to)


def spread(group, src, dst, send, recv):
    copies = []
    for d, j in group.others():
        cp = remote(src(j), dst(group.me), send.at[d], recv.at[group.me], group.address(j))
        cp.start()
        copies.append(cp)
    return copies


def arrived(group, src, dst, send, recv):
    for d, j in group.others():
        remote(src(j), dst(j), send.at[d], recv.at[j], group.address(j)).wait_recv()


def fetch_kernel(n, ny, wanted, table, slots, lengths, x0, ids_in, words_out,
                 ids_sm, sendbuf, cache, words, wordst, rowcode, rowbit, colcode, colbit, acc,
                 id_send, id_recv, row_send, row_recv, sm_sem, words_sem):
    nz = n // ny
    cap, emb = cache.shape[1:]
    feats, bag, samples = slots.shape
    me = lax.axis_index("shard")
    z = me // ny
    barrier = pltpu.get_barrier_semaphore()

    @pl.loop(0, n - 1)
    def _(k):
        pl.semaphore_signal(barrier, inc=1, device_id={"shard": peer_of(k, me, ny, nz)})

    pl.semaphore_wait(barrier, n - 1)

    def id_copy(p, slot):
        return remote(wanted.at[p], ids_in.at[slot], id_send.at[p], id_recv.at[slot], {"shard": p})

    def row_copy(p, slot):
        return remote(sendbuf.at[p], cache.at[slot], row_send.at[p], row_recv.at[slot], {"shard": p})

    @pl.loop(0, n - 1)
    def _(k):
        id_copy(peer_of(k, me, ny, nz), me).start()

    ids_in[me] = wanted[me]
    key_codes(slots, lengths, rowcode, rowbit)
    colcode[...] = rowcode[...].T
    colbit[...] = rowbit[...].T

    @pl.loop(0, n - 1)
    def _(k):
        p = peer_of(k, me, ny, nz)
        id_copy(p, p).wait_recv()

    to_smem = pltpu.make_async_copy(ids_in, ids_sm, sm_sem)
    to_smem.start()
    to_smem.wait()

    def serve(p, out):
        @pl.loop(0, cap // 16)
        def _(t):
            for i in range(16):
                row = t * 16 + i
                out[p, pl.ds(row, 1), :] = table[pl.ds(ids_sm[p, 0, row], 1), :]

    @pl.loop(0, n - 1)
    def _(k):
        p = peer_of(k, me, ny, nz)
        serve(p, sendbuf)
        row_copy(p, me).start()

    serve(me, cache)

    count_words(
        words, feats, bag, lambda key: colcode[:, key:key + 1], lambda key: colbit[:, key:key + 1],
        lax.broadcasted_iota(I32, (samples, cap), 1))

    @pl.loop(0, feats)
    def _(f):
        acc[f] = jnp.zeros(acc.shape[1:], F32)

    count_words(
        wordst, feats, bag, lambda key: rowcode[key:key + 1, :], lambda key: rowbit[key:key + 1, :],
        lax.broadcasted_iota(I32, (cap, samples), 0))
    words_copy = pltpu.make_async_copy(wordst, words_out, words_sem)
    words_copy.start()

    @pl.loop(0, nz)
    def _(j):
        first = plane_from(plane_step(j, nz), z, nz) * ny

        @pl.loop(0, ny)
        def _(i):
            p = first + i

            @pl.when(p != me)
            def _():
                row_copy(p, p).wait_recv()

        rhs = jnp.concatenate(
            [split(cache[first + i] * nibble_scale(first + i)) for i in range(ny)], axis=0)

        @pl.loop(0, feats)
        def _(f):
            word = words[first // 8, f]
            lhs = jnp.concatenate([counts(word, first + i) for i in range(ny)], axis=1)
            acc[f] = acc[f] + dot(lhs, rhs, NN)

    for f in range(feats):
        x0[:, f * emb:(f + 1) * emb] = (acc[f, :, :emb] + acc[f, :, emb:]).astype(BF16)

    @pl.loop(0, n - 1)
    def _(k):
        p = peer_of(k, me, ny, nz)
        id_copy(p, me).wait_send()
        row_copy(p, me).wait_send()

    words_copy.wait()


def fetch(wanted, table, slots, lengths, ny):
    n, cap = wanted.shape
    emb = table.shape[1]
    feats, bag, samples = slots.shape
    keys = feats * bag
    vm = pl.BlockSpec(memory_space=pltpu.VMEM)
    dma = pltpu.SemaphoreType.DMA
    return pl.pallas_call(
        functools.partial(fetch_kernel, n, ny),
        out_shape=[
            jax.ShapeDtypeStruct((samples, feats * emb), BF16),
            jax.ShapeDtypeStruct((n, 1, cap), I32),
            jax.ShapeDtypeStruct((pl.cdiv(n, 8), feats, cap, samples), I32),
        ],
        in_specs=[vm] * 4,
        out_specs=[vm, vm, pl.BlockSpec(memory_space=pl.ANY)],
        scratch_shapes=[
            pltpu.SMEM((n, 1, cap), I32),
            pltpu.VMEM((n, cap, emb), F32),
            pltpu.VMEM((n, cap, emb), F32),
            pltpu.VMEM((pl.cdiv(n, 8), feats, samples, cap), I32),
            pltpu.VMEM((pl.cdiv(n, 8), feats, cap, samples), I32),
            pltpu.VMEM((keys, samples), I32),
            pltpu.VMEM((keys, samples), I32),
            pltpu.VMEM((samples, keys), I32),
            pltpu.VMEM((samples, keys), I32),
            pltpu.VMEM((feats, samples, 2 * emb), F32),
            dma((n,)), dma((n,)), dma((n,)), dma((n,)), dma, dma,
        ],
        compiler_params=pltpu.CompilerParams(
            collective_id=0, has_side_effects=True, vmem_limit_bytes=VMEM_LIMIT),
        name="fetch_pool",
    )(wanted.reshape(n, 1, cap), table, slots, lengths)


def add_refs(out, parts, chunk):
    count = out.shape[0]
    chunk = math.gcd(chunk, count)

    @pl.loop(0, count // chunk)
    def _(t):
        w = pl.ds(t * chunk, chunk)
        total = parts[0][w]
        for p in parts[1:]:
            total = total + p[w]
        out[w] = total


def shares(r, nx, ny):
    per = r // 2
    unit = nx * ny
    second = max(unit, per // 2 // unit * unit)
    return per - second, second


class Stream:
    def __init__(self, local, out, start, size, core, first, second, gz, bufs, sems):
        self.local, self.out, self.start, self.size = local, out, start, size
        self.core, self.first, self.second, self.gz = core, first, second, gz
        self.r1, self.r2, self.b, self.r3, self.c, self.r4 = bufs
        self.sems = sems
        self.share = local.shape[0] // 2
        self.piece = size // first.size
        self.unit = self.piece // second.size
        self.pending = []

    def pair(self, k):
        return self.sems[0].at[k], self.sems[1].at[k]

    def go(self, group, src, dst, k):
        self.pending += spread(group, src, dst, *self.pair(k))

    def come(self, group, src, dst, k):
        arrived(group, src, dst, *self.pair(k))

    def half(self, ref, c):
        return ref.at[pl.ds(c * self.share + self.start, self.size)]

    def core_args(self):
        return self.core, lambda j: self.half(self.local, j), lambda i: self.r1, 0

    def first_args(self):
        return self.first, lambda j: self.r1.at[pl.ds(j * self.piece, self.piece)], lambda i: self.r2.at[i], 1

    def second_args(self):
        return self.second, lambda j: self.b.at[pl.ds(j * self.unit, self.unit)], lambda i: self.r3.at[i], 2

    def z_args(self):
        return self.gz, lambda j: self.c.at[:, j], lambda i: self.r4.at[i], 3

    def at(self, a=None, bb=None):
        at = self.core.me * self.share + self.start
        if a is not None:
            at = at + a * self.piece
        if bb is not None:
            at = at + bb * self.unit
        return at

    def zback_args(self):
        here = lambda i: self.out.at[pl.ds(self.at(self.first.me, self.second.me), self.unit), i]
        return self.gz, lambda j: here(self.gz.me), here, 4

    def second_back_args(self):
        here = lambda i: self.out.at[pl.ds(self.at(self.first.me, i), self.unit)]
        return self.second, lambda j: here(self.second.me), here, 5

    def first_back_args(self):
        here = lambda i: self.out.at[pl.ds(self.at(i), self.piece)]
        return self.first, lambda j: here(self.first.me), here, 6

    def core_back_args(self):
        here = lambda i: self.half(self.out, i)
        return self.core, lambda j: here(self.core.me), here, 7

    def step(self, k):
        args = (self.core_args, self.first_args, self.second_args, self.z_args,
                self.zback_args, self.second_back_args, self.first_back_args, self.core_back_args)
        if k >= 0:
            group, src, dst, i = args[k]()
            self.come(group, src, dst, i)
            if k == 0:
                add_refs(self.r1, [self.r1, self.half(self.local, group.me)], 4)
            elif k < 4:
                out = (None, self.b, self.c, None)[k]
                if k == 3:
                    out = self.out.at[pl.ds(self.at(self.first.me, self.second.me), self.unit), self.gz.me]
                add_refs(out, [src(group.me)] + [dst(j) for _, j in group.others()], 2)
        if k + 1 < len(args):
            self.go(*args[k + 1]())


def dense_kernel(nx, ny, nz, x0, words_in, cot, cw, cb, tw, tb, ow, served,
                 logits, table_out, cross_hbm, top_hbm, small_out,
                 cross_out, top_out,
                 g_cross, g_top, small, slot_grads, back, tsum, rt1, rt2,
                 words, y, h, dzb, dyb, dh, dxhl, bufs, sm_bufs, sems):
    n = ny * nz
    cap, emb = back.shape[1:]
    rows = tsum.shape[0]
    feats, samples = dxhl.shape[:2]
    width, top = tw.shape
    dp, me = lax.axis_index("dp"), lax.axis_index("shard")
    x, core, z, yy = dp // 2, dp % 2, me // ny, me % ny
    gx = Group(nx, x, lambda j: {"dp": j * 2 + core})
    gy = Group(ny, yy, lambda j: {"shard": z * ny + j})
    gz = Group(nz, z, lambda j: {"shard": j * ny + yy})
    gc = Group(2, core, lambda j: {"dp": x * 2 + j})
    g_send, g_recv, t_send, t_recv, sm_send, sm_recv, d_send, d_recv, words_sem, out_sems = sems
    words_copy = pltpu.make_async_copy(words_in, words, words_sem)
    words_copy.start()

    barrier = pltpu.get_barrier_semaphore()

    @pl.loop(0, n - 1)
    def _(k):
        pl.semaphore_signal(barrier, inc=1, device_id={"shard": peer_of(k, me, ny, nz)})

    for grp in (gx, gc):
        for _, j in grp.others():
            pl.semaphore_signal(barrier, inc=1, device_id=grp.address(j))

    streams = []
    for a, (local, out) in enumerate(((g_top, top_out), (g_cross, cross_out))):
        for hh in range(2):
            first, second = ((gx, gy), (gy, gx))[hh]
            s = 2 * a + hh
            part = shares(local.shape[0], nx, ny)
            streams.append(Stream(local, out, hh * part[0], part[hh], gc, first, second, gz, bufs[6 * s:6 * s + 6],
                                  (d_send.at[s], d_recv.at[s])))
    tops, crosses = streams[:2], streams[2:]

    step = min(256, width)
    lanes = step // 128

    def put_small(at, vec):
        for t in range(lanes):
            small[pl.ds(at + t, 1), :] = vec[:, t * 128:(t + 1) * 128]

    def put_dense(out, j, val):
        per = val.shape[1] // 128
        deep = nz // per
        count = step // 8 // deep
        for t in range(per):
            v = val[:, t * 128:(t + 1) * 128].reshape(count, deep, 8, 128)
            for i in range(deep):
                out[pl.ds(j * count, count), i * per + t] = v[:, i]

    @pl.loop(0, width // step)
    def _(j):
        c = pl.ds(pl.multiple_of(j * step, step), step)
        yv = dot(x0[...], cw[:, c], NN) + cb[:, c]
        y[:, c] = yv
        xf = x0[:, c].astype(F32)
        h[:, c] = (xf * yv + xf).astype(BF16)

    cotb = jnp.broadcast_to(cot[...], (128, samples)).T
    lsum = jnp.zeros((samples, 128), F32)
    tstep = min(256, top)
    for j in range(top // tstep):
        c = pl.ds(j * tstep, tstep)
        zv = dot(h[...], tw[:, c], NN) + tb[:, c]
        sig = jax.nn.sigmoid(zv)
        u = zv * sig
        uw = u * ow[:, c]
        cotw = jnp.concatenate([cotb] * (tstep // 128), axis=1)
        for t in range(tstep // 128):
            lsum = lsum + uw[:, t * 128:(t + 1) * 128]
        gow = jnp.sum(u * cotw, axis=0, keepdims=True)
        dz = cotw * ow[:, c] * (sig * (1.0 + zv * (1.0 - sig)))
        gtb = jnp.sum(dz, axis=0, keepdims=True)
        for t in range(tstep // 128):
            at = width // 128 + j * (tstep // 128) + t
            small[pl.ds(at, 1), :] = gtb[:, t * 128:(t + 1) * 128]
            small[pl.ds(at + top // 128, 1), :] = gow[:, t * 128:(t + 1) * 128]
        dzb[:, c] = dz.astype(BF16)
    logits[...] = jnp.sum(lsum.T, axis=0, keepdims=True)

    @pl.loop(0, width // step)
    def _(j):
        c = pl.ds(pl.multiple_of(j * step, step), step)
        put_dense(g_top, j, dot(h[:, c], dzb[...], TN))

    pl.semaphore_wait(barrier, n - 1 + nx - 1 + 1)
    for s in tops:
        s.step(-1)

    @pl.loop(0, width // step)
    def _(j):
        c = pl.ds(pl.multiple_of(j * step, step), step)
        dhv = dot(dzb[...], tw[c, :], NT)
        dh[:, c] = dhv
        dy = dhv * x0[:, c].astype(F32)
        put_small(j * lanes, jnp.sum(dy, axis=0, keepdims=True))
        dyb[:, c] = dy.astype(BF16)

    @pl.loop(0, width // step)
    def _(j):
        c = pl.ds(pl.multiple_of(j * step, step), step)
        put_dense(g_cross, j, dot(x0[:, c], dyb[...], TN))

    for s in crosses:
        s.step(-1)
    pending = []
    s_core, s_x, s_y, s_z, sm1, sm2, sm3 = sm_bufs

    def small_go(k, grp, src, slots_):
        slots_[grp.me] = src[...]
        args = (grp, lambda j: src, lambda i: slots_.at[i], sm_send.at[k], sm_recv.at[k])
        pending.extend(spread(*args))
        return args

    def small_come(args, slots_, out):
        arrived(*args)
        total = slots_[0]
        for i in range(1, slots_.shape[0]):
            total = total + slots_[i]
        out[...] = total

    sm_args = small_go(0, gc, small, s_core)

    @pl.loop(0, width // step)
    def _(j):
        c = pl.ds(pl.multiple_of(j * step, step), step)
        dx = dh[:, c] * (y[:, c] + 1.0) + dot(dyb[...], cw[c, :], NT)
        for t in range(step // emb):
            dxhl[j * (step // emb) + t] = split(dx[:, t * emb:(t + 1) * emb])

    for s in tops:
        s.step(0)
    words_copy.wait()
    for s in crosses:
        s.step(0)
    small_come(sm_args, s_core, sm1)
    sm_args = small_go(1, gx, sm1, s_x)

    def grad_copy(p, slot):
        return remote(slot_grads.at[p], back.at[slot], g_send.at[p], g_recv.at[slot], {"shard": p})

    def plane_to(j):
        return ((z + far_step(j, nz)) % nz) * ny

    def slot_plane(j):
        first = plane_to(j)
        total = jnp.zeros((ny * cap, 2 * emb), F32)
        for f in range(feats):
            word = words[first // 8, f]
            lhs = jnp.concatenate([counts(word, first + i) for i in range(ny)], axis=0)
            total = total + dot(lhs, dxhl[f], NN)
        for i in range(ny):
            part = total[i * cap:(i + 1) * cap]
            slot_grads[first + i] = (part[:, :emb] + part[:, emb:]) * nibble_scale(first + i)

    def send_plane(j):
        @pl.loop(0, ny)
        def _(i):
            p = plane_to(j) + (yy + i + 1) % ny

            @pl.when(p != me)
            def _():
                grad_copy(p, me).start()

        @pl.when(j == nz - 1)
        def _():
            back[me] = slot_grads[me]

    def owner_plane(j):
        first = plane_from(far_step(j, nz), z, nz) * ny

        @pl.loop(0, ny)
        def _(i):
            p = first + i

            @pl.when(p != me)
            def _():
                grad_copy(p, p).wait_recv()

        rhs = jnp.concatenate([split(back[first + i]) for i in range(ny)], axis=0)
        ids = jnp.concatenate([served[first + i] for i in range(ny)], axis=1)
        mstep = min(512, rows)

        @pl.loop(0, rows // mstep)
        def _(t):
            at = t * mstep
            row = lax.broadcasted_iota(I32, (mstep, ny * cap), 0) + at
            hot = jnp.where(row == ids, F32(1), F32(0)).astype(BF16)
            part = dot(hot, rhs, NN)
            part = part[:, :emb] + part[:, emb:]
            w = pl.ds(pl.multiple_of(at, mstep), mstep)
            tsum[w] = jnp.where(j == 0, part, tsum[w] + part)

    def slot_planes(lo, hi, send):
        @pl.loop(lo, min(hi, nz))
        def _(j):
            slot_plane(j)
            if send:
                send_plane(j)

    def send_planes(lo, hi):
        @pl.loop(lo, min(hi, nz))
        def _(j):
            send_plane(j)

    def owner_planes(lo, hi):
        @pl.loop(lo, min(hi, nz))
        def _(j):
            owner_plane(j)

    def steps(which, k):
        for s in which:
            s.step(k)

    early = min(3, nz)
    slot_planes(0, early, True)
    steps(tops, 1)
    slot_planes(early, 4, False)
    steps(crosses, 1)
    small_come(sm_args, s_x, sm2)
    sm_args = small_go(2, gy, sm2, s_y)
    steps(tops, 2)
    slot_planes(min(4, nz), 6, False)
    steps(crosses, 2)
    small_come(sm_args, s_y, sm3)
    sm_args = small_go(3, gz, sm3, s_z)
    slot_planes(min(6, nz), nz, False)
    steps(tops, 3)
    steps(crosses, 3)
    send_planes(early, nz)
    steps(tops, 4)
    steps(crosses, 4)
    owner_planes(0, early)
    steps(tops, 5)
    steps(crosses, 5)
    small_come(sm_args, s_z, small_out)
    owner_planes(early, 5)
    steps(tops, 6)
    owner_planes(min(5, nz), nz)

    thalf = rows // 2
    tq = thalf // nx
    rows_at = lambda ref, at, size: ref.at[pl.ds(pl.multiple_of(at, size), size)]
    tside = lambda ref, i: rows_at(ref, i * thalf, thalf)
    tpart = lambda ref, i: rows_at(ref, i * tq, tq)
    sem = lambda k: (t_send.at[k], t_recv.at[k])
    tc = (gc, lambda j: tside(tsum, j), lambda i: rt1, *sem(0))
    pending += spread(*tc)
    arrived(*tc)
    rt1[...] = rt1[...] + tside(tsum, core)[...]
    tx = (gx, lambda j: tpart(rt1, j), lambda i: rt2.at[i], *sem(1))
    pending += spread(*tx)
    for s in crosses:
        s.step(6)
    arrived(*tx)
    mine = tpart(tside(table_out, core), x)
    total = tpart(rt1, x)[...]
    for _, j in gx.others():
        total = total + rt2[j]
    mine[...] = total
    there = lambda i: rows_at(table_out, core * thalf + i * tq, tq)
    tb_ = (gx, lambda j: there(x), there, *sem(2))
    pending += spread(*tb_)
    flushes = []
    for i, (which, src, dst) in enumerate(((tops, top_out, top_hbm), (crosses, cross_out, cross_hbm))):
        steps(which, 7)
        flushes.append(pltpu.make_async_copy(src, dst, out_sems.at[i]))
        flushes[-1].start()
    arrived(*tb_)
    tcb = (gc, lambda j: tside(table_out, core), lambda i: tside(table_out, i), *sem(3))
    pending += spread(*tcb)
    arrived(*tcb)
    for cp in flushes:
        cp.wait()

    for cp in pending + [cp for s in streams for cp in s.pending]:
        cp.wait_send()

    @pl.loop(0, n - 1)
    def _(k):
        grad_copy(peer_of(k, me, ny, nz), me).wait_send()


def dense_and_reduce(x0, words, cot, cw, cb, tw, tb, ow, served, nx, ny, rows):
    samples, width = x0.shape
    top = tw.shape[1]
    feats = words.shape[1]
    n, _, cap = served.shape
    emb = width // feats
    nz = n // ny
    vm = pl.BlockSpec(memory_space=pltpu.VMEM)
    v = pltpu.VMEM
    dma = lambda *s: pltpu.SemaphoreType.DMA(s)
    tiles = lambda *lead: (*lead, 8, 128)
    r_cross = width // 8 * (width // 128) // nz
    r_top = width // 8 * (top // 128) // nz
    sm = ((width + 2 * top) // 128, 128)
    most = max(nx, ny, nz)

    bufs = []
    for r in (r_top, r_cross):
        for (a, b), q in zip(((nx, ny), (ny, nx)), shares(r, nx, ny)):
            p = q // a
            u = p // b
            bufs += [v(tiles(q, nz), F32), v(tiles(a, p, nz), F32), v(tiles(p, nz), F32),
                     v(tiles(b, u, nz), F32), v(tiles(u, nz), F32), v(tiles(nz, u), F32)]
    sm_bufs = [v((k, *sm), F32) for k in (2, nx, ny, nz)] + [v(sm, F32)] * 3
    sems = [dma(n), dma(n), dma(4, most), dma(4, most), dma(4, most), dma(4, most), dma(4, 8, most), dma(4, 8, most),
            pltpu.SemaphoreType.DMA, dma(2)]
    own = [
        v(tiles(r_cross, nz), F32), v(tiles(r_top, nz), F32),
        v(tiles(r_cross, nz), F32), v(tiles(r_top, nz), F32), v(sm, F32),
        v((n, cap, emb), F32), v((n, cap, emb), F32), v((rows, emb), F32),
        v((rows // 2, emb), F32), v((nx, rows // 2 // nx, emb), F32),
        v(words.shape, I32),
        v((samples, width), F32), v((samples, width), BF16), v((samples, top), BF16), v((samples, width), BF16),
        v((samples, width), F32), v((feats, samples, 2 * emb), BF16),
    ]

    def body(*refs):
        head, rest = refs[:14 + len(own)], refs[14 + len(own):]
        dense_kernel(nx, ny, nz, *head, rest[:24], rest[24:31], rest[31:])

    return pl.pallas_call(
        body,
        out_shape=[
            jax.ShapeDtypeStruct((1, samples), F32),
            jax.ShapeDtypeStruct((rows, emb), F32),
            jax.ShapeDtypeStruct(tiles(r_cross, nz), F32),
            jax.ShapeDtypeStruct(tiles(r_top, nz), F32),
            jax.ShapeDtypeStruct(sm, F32),
        ],
        in_specs=[vm, pl.BlockSpec(memory_space=pl.ANY)] + [vm] * 7,
        out_specs=[vm, vm, pl.BlockSpec(memory_space=pl.ANY), pl.BlockSpec(memory_space=pl.ANY), vm],
        scratch_shapes=own + bufs + sm_bufs + sems,
        compiler_params=pltpu.CompilerParams(
            collective_id=1, has_side_effects=True, vmem_limit_bytes=VMEM_LIMIT),
        name="dense_reduce",
    )(x0, words, cot, cw, cb, tw, tb, ow, served)


def publish_kernel(pieces, cross, tops, table, small, logits, cross_out, top_out, table_out,
                   cb_out, tb_out, ow_out, logits_out, cross_buf, top_buf, table_buf, sems):
    logits_out[...] = logits[...]
    reads, writes = [], []
    for src, buf, dst in ((cross, cross_buf, cross_out), (tops, top_buf, top_out), (table, table_buf, table_out)):
        size = src.shape[0] // pieces
        for i in range(pieces):
            w = pl.ds(i * size, size)
            k = len(reads)
            reads.append(pltpu.make_async_copy(src.at[w], buf.at[w], sems.at[0, k]))
            writes.append(pltpu.make_async_copy(buf.at[w], dst.at[w], sems.at[1, k]))
    for read in reads:
        read.start()
    for read, write in zip(reads, writes):
        read.wait()
        write.start()
    at = 0
    for out in (cb_out, tb_out, ow_out):
        out[...] = small[pl.ds(at, out.shape[0]), :]
        at += out.shape[0]
    for write in writes:
        write.wait()


def publish(cross, tops, table, small, logits, width, top):
    hbm = pl.BlockSpec(memory_space=pl.ANY)
    vm = pl.BlockSpec(memory_space=pltpu.VMEM)
    pieces = 4
    return pl.pallas_call(
        functools.partial(publish_kernel, pieces),
        out_shape=[jax.ShapeDtypeStruct(a.shape, F32) for a in (cross, tops, table)]
        + [jax.ShapeDtypeStruct((k // 128, 128), F32) for k in (width, top, top)]
        + [jax.ShapeDtypeStruct(logits.shape, F32)],
        in_specs=[hbm, hbm, hbm, vm, vm],
        out_specs=[hbm, hbm, hbm, vm, vm, vm, vm],
        scratch_shapes=[pltpu.VMEM(a.shape, F32) for a in (cross, tops, table)]
        + [pltpu.SemaphoreType.DMA((2, 3 * pieces))],
        compiler_params=pltpu.CompilerParams(vmem_limit_bytes=VMEM_LIMIT),
        name="publish",
    )(cross, tops, table, small, logits)


def from_tiles(tiles, rows, columns):
    return jnp.transpose(tiles.reshape(rows // 8, columns // 128, 8, 128), (0, 2, 1, 3)).reshape(rows, columns)


def on_device(table, cross_weight, cross_bias, top_weight, top_bias, out_weight, wanted, slots, lengths, logit_grad,
              nx=NX, ny=NY):
    width, top = top_weight.shape
    keys, live = jnp.transpose(slots, (1, 2, 0)), lengths.T
    x0, served, words = fetch(wanted[0], table, keys, live, ny)
    logits, table_grad, cross, tops, vecs = dense_and_reduce(
        x0, words, logit_grad[None], cross_weight, cross_bias[None], top_weight, top_bias[None], out_weight[None],
        served, nx, ny, table.shape[0])
    cross, tops, table_grad, g_cb, g_tb, g_ow, logits = publish(
        cross, tops, table_grad, vecs, logits, width, top)
    return (logits[0], from_tiles(cross, width, width), from_tiles(tops, width, top),
            g_cb.reshape(-1), g_tb.reshape(-1), g_ow.reshape(-1), table_grad)


def solution(mesh):
    placed = (
        P("shard", None),
        P(),
        P(),
        P(),
        P(),
        P(),
        P(("dp", "shard"), None, None),
        P(("dp", "shard"), None, None),
        P(("dp", "shard"), None),
        P(("dp", "shard")),
    )
    return jax.shard_map(
        on_device,
        mesh=mesh,
        in_specs=placed,
        out_specs=(P(("dp", "shard")), P(), P(), P(), P(), P(), P("shard", None)),
        check_vma=False,
    )
```
